128 devices in a mesh: freq: 8 (over z, core), rcv: 16 (over x, y).
Axes of the slice: x: 4, y: 4, z: 4, core: 2. Of those that a mesh axis runs over, the one named last changes fastest.
Arguments:
- spectra: float32 [128, 2, 512, 512], P('freq', None, 'rcv'), may hold values from -0.5 to 0.5
- counts: int32 [8], replicated, may hold values from 1 to 16, 64 in all
- partner: int32 [512], replicated, may hold values from 0 to 511, as said below
- recorded: float32 [512, 512, 512], P('freq', 'rcv'), may hold values from -3 to 3
- gain_index: int32 [512, 512], P('freq', 'rcv'), may hold values from 0 to 15
- gain_table: float32 [2, 16], replicated, may hold values from 0.5 to 1.5
Outputs:
- primaries: float32 [512, 512, 512], P('freq', 'rcv')
The draws below stay inside these ranges and needn't reach their ends.
Inputs may be any that keep to these rules, and one draw needn't show every extreme that they name: `counts`: the bands hold 64 frequencies together, and some band holds exactly 16. `partner`: A permutation that maps each aligned block of 32 indices onto itself.
All inputs are finite; a program needn't handle non-finite values.
Results may differ from the reference program's by a relative error of at most 0.00005.
Values sent between devices are 32-bit elements; how exact they have to be, the bound alone decides.
A program may use at most 128 MiB of HBM per device.

```python
import math
import jax
import jax.numpy as jnp
import numpy as np
from jax import lax

SIDE = 512
NT = 512
LEVELS = 16
FCAP = 16
NF = 64
SLOTS = 128
RT = 32
N_FREQ = 8


def draw_partner(key, part):
    block_count = SIDE // RT
    block_keys = jax.random.split(jax.random.fold_in(key, 11), block_count)
    shuffled = jax.vmap(lambda one_key: jax.random.permutation(one_key, RT))(block_keys)
    starts = jnp.arange(block_count, dtype=jnp.int32)[:, None] * RT
    return (shuffled.astype(jnp.int32) + starts).reshape(SIDE)


def touch_ends(result, rng, smallest, top_value):
    shape = result.shape
    index_at = [jax.random.randint(jax.random.fold_in(rng, axis), (), 0, shape[axis]) for axis in range(len(shape))]
    result = result.at[tuple(index_at)].set(smallest)
    longest = shape.index(max(shape))
    index_at[longest] = (index_at[longest] + 1) % shape[longest]
    return result.at[tuple(index_at)].set(top_value)


def steps_of(key, extent, pieces, smallest, largest):
    gain = 1.0
    for position, blocks in pieces:
        heights = jax.random.uniform(jax.random.fold_in(jax.random.fold_in(key, 6), position), (blocks,), jnp.float32, smallest / len(pieces), largest / len(pieces))
        gain = gain * jnp.repeat(jnp.exp(heights), extent[position] // blocks).reshape((-1,) + (1,) * (len(extent) - 1 - position))
    return gain


def split_up(count, total, reach, lean):
    portions = [(1 << 20) // math.isqrt(rank ** lean) + 1 for rank in range(2, count + 1)]
    spare, given = total - reach - (count - 1), [1] * (count - 1)
    while spare > 0:
        candidates = [i for i in range(count - 1) if given[i] < reach]
        mass, budget = sum([portions[i] for i in candidates]), spare
        for i in candidates:
            extra = min(reach - given[i], max(1, budget * portions[i] // mass), spare)
            given[i] = given[i] + extra
            spare = spare - extra
    return np.array([reach] + given)


def uneven(key, amount, total, most, lean):
    if amount == 2:
        one = jax.random.randint(key, (), max(1, total - most), min(most, total - 1) + 1)
        return jnp.stack([one, total - one])
    sizes = jnp.asarray(split_up(amount, total, most, lean), jnp.int32)
    couples = (amount - 1) // 2
    source_of, receiver = sizes[1:1 + 2 * couples:2], sizes[2:2 + 2 * couples:2]
    room = jnp.minimum(source_of - 1, most - receiver)
    shifted = jax.random.randint(jax.random.fold_in(key, 1), (couples,), 0, 1 << 20) % (room + 1)
    sizes = sizes.at[1:1 + 2 * couples:2].set(source_of - shifted).at[2:2 + 2 * couples:2].set(receiver + shifted)
    return sizes[jax.random.permutation(jax.random.fold_in(key, 2), amount)]


def noise(key, extent, scale, most, pieces=(), kind=jnp.bfloat16):
    array = scale * jax.random.normal(key, extent, jnp.float32)
    if pieces:
        array = array * steps_of(key, extent, pieces, -0.22, 0.18)
    return jnp.clip(array, -most, most).astype(kind)


def setup_inputs(seed: int = 0) -> dict:
    streams_of = jax.random.split(jax.random.key(seed), 7)
    return {
        "spectra": noise(streams_of[0], (SLOTS, 2, SIDE, SIDE), 0.0625, 0.5, ((0, 8), (2, 16)), jnp.float32),
        "counts": uneven(streams_of[1], N_FREQ, NF, FCAP, 2).astype(jnp.int32),
        "partner": draw_partner(jax.random.fold_in(streams_of[6], 71), 0),
        "recorded": noise(streams_of[3], (SIDE, SIDE, NT), 0.5, 3.0, ((0, 8), (1, 16)), jnp.float32),
        "gain_index": touch_ends(jax.random.randint(streams_of[4], (SIDE, SIDE), 0, LEVELS), jax.random.fold_in(streams_of[4], 1), 0, LEVELS - 1).astype(jnp.int32),
        "gain_table": jnp.clip(jax.random.uniform(streams_of[5], (2, LEVELS), jnp.float32, 0.5, 1.5), 0.5, 1.5),
    }


def complex_product(left_real, left_imag, right_real, right_imag):
    highest = lax.Precision.HIGHEST
    real_part = jnp.dot(left_real, right_real, precision=highest, preferred_element_type=jnp.float32) - jnp.dot(left_imag, right_imag, precision=highest, preferred_element_type=jnp.float32)
    imag_part = jnp.dot(left_real, right_imag, precision=highest, preferred_element_type=jnp.float32) + jnp.dot(left_imag, right_real, precision=highest, preferred_element_type=jnp.float32)
    return real_part, imag_part


def mirrored(matrix, partner, inverse):
    return jnp.swapaxes(matrix[:, partner, :][:, :, inverse], 1, 2)


def time_table(bin_numbers, samples):
    phases = (bin_numbers[:, None] * jnp.arange(samples, dtype=jnp.int32)[None, :]) % samples
    angles = (2.0 * jnp.pi / samples) * phases.astype(jnp.float32)
    return jnp.stack([jnp.cos(angles), -jnp.sin(angles)], axis=1)


def reference(spectra, counts, partner, recorded, gain_index, gain_table):
    highest = lax.Precision.HIGHEST
    slot_total = spectra.shape[0]
    capacity = slot_total // N_FREQ
    offsets = jnp.cumsum(counts) - counts
    slot_ids = jnp.arange(slot_total, dtype=jnp.int32)
    band_of = slot_ids // capacity
    within = slot_ids % capacity
    slot_live = within < counts[band_of]
    bin_numbers = offsets[band_of] + within + 1
    masked = jnp.where(slot_live[:, None, None, None], spectra, jnp.zeros((), spectra.dtype))
    inverse = jnp.zeros_like(partner).at[partner].set(jnp.arange(partner.shape[0], dtype=jnp.int32))

    def one_slot(matrix):
        first_real, first_imag = complex_product(matrix[0], matrix[1], matrix[0], matrix[1])
        second_real, second_imag = complex_product(first_real, first_imag, matrix[0], matrix[1])
        first_order = jnp.stack([first_real, first_imag])
        second_order = jnp.stack([second_real, second_imag])
        first_avg = 0.5 * (first_order + mirrored(first_order, partner, inverse))
        second_avg = 0.5 * (second_order + mirrored(second_order, partner, inverse))
        return first_avg, second_avg

    first_all, second_all = lax.map(one_slot, masked)
    phase_table = time_table(bin_numbers, NT)
    first_time = jnp.einsum("fcrs,fct->srt", first_all, phase_table, precision=highest)
    second_time = jnp.einsum("fcrs,fct->srt", second_all, phase_table, precision=highest)
    choose = (gain_index[:, :, None] == jnp.arange(LEVELS, dtype=jnp.int32)).astype(jnp.float32)
    gain_first = jnp.sum(choose * gain_table[0], axis=-1)
    gain_second = jnp.sum(choose * gain_table[1], axis=-1)
    return recorded - gain_first[:, :, None] * first_time - gain_second[:, :, None] * second_time
```

```python
import functools

import jax
import jax.numpy as jnp
import numpy as np
from jax import lax
from jax.experimental import pallas as pl
from jax.experimental.pallas import tpu as pltpu
from jax.sharding import PartitionSpec as P

MESH = pl.DeviceIdType.MESH
ANY = pl.BlockSpec(memory_space=pl.ANY)
VMEM = pl.BlockSpec(memory_space=pltpu.VMEM)
SMEM = pl.BlockSpec(memory_space=pltpu.SMEM)

NT = 512
SIDE = 512
LIVE = 64
NP = 8
NQ = 16
F32 = jnp.float32
BF16 = jnp.bfloat16


def basis():
    bins = np.arange(1, LIVE + 1, dtype=np.int64)[:, None]
    angles = 2.0 * np.pi / NT * ((bins * np.arange(NT, dtype=np.int64)[None, :]) % NT)
    table = np.concatenate([np.cos(angles), -np.sin(angles)], axis=0).astype(np.float32)
    high = table.astype(BF16)
    low = (table - high.astype(np.float32)).astype(BF16)
    return np.concatenate([high, high, low], axis=0)


def halves(x):
    high = x.astype(BF16)
    return high, (x - high.astype(F32)).astype(BF16)


def gather_kernel(spec, gtile, whole, gains, own_sem, send_sem, recv_sem, gown_sem, gsend_sem, grecv_sem):
    p, q = lax.axis_index("freq"), lax.axis_index("rcv")
    barrier = pltpu.get_barrier_semaphore()

    def greet_q(t, _):
        pl.semaphore_signal(barrier, inc=1, device_id=(p, lax.rem(q + t, NQ)), device_id_type=MESH)
        return 0

    def greet_p(t, _):
        pl.semaphore_signal(barrier, inc=1, device_id=(lax.rem(p + t, NP), q), device_id_type=MESH)
        return 0

    lax.fori_loop(1, NQ, greet_q, 0)
    lax.fori_loop(1, NP, greet_p, 0)
    gcopy = pltpu.make_async_copy(gtile, gains.at[p, q], gown_sem)
    gcopy.start()
    own = pltpu.make_async_copy(spec.at[q], whole.at[:, pl.ds(q * 32, 32), :], own_sem)
    own.start()
    pl.semaphore_wait(barrier, NQ + NP - 2)

    def gain_q(t):
        return pltpu.make_async_remote_copy(
            gtile, gains.at[p, q], gsend_sem.at[t], grecv_sem.at[t],
            device_id=(p, lax.rem(q + t, NQ)), device_id_type=MESH)

    def gain_p(t):
        return pltpu.make_async_remote_copy(
            gains.at[p], gains.at[p], gsend_sem.at[NQ + t], grecv_sem.at[NQ + t],
            device_id=(lax.rem(p + t, NP), q), device_id_type=MESH)

    def rows(t):
        k = lax.rem(q + t, NQ)
        return pltpu.make_async_remote_copy(
            spec.at[k], whole.at[:, pl.ds(q * 32, 32), :], send_sem.at[t], recv_sem.at[t],
            device_id=(p, k), device_id_type=MESH)

    def loop(first, last, fn):
        def body(t, _):
            fn(t)
            return 0
        lax.fori_loop(first, last, body, 0)

    loop(1, NQ, lambda t: gain_q(t).start())
    loop(1, NQ, lambda t: rows(t).start())
    gcopy.wait()
    loop(1, NQ, lambda t: gain_q(t).wait())
    loop(1, NP, lambda t: gain_p(t).start())
    own.wait()
    loop(1, NQ, lambda t: rows(t).wait())
    loop(1, NP, lambda t: gain_p(t).wait())


def gather_rows(spectra, gtile):
    dma = pltpu.SemaphoreType.DMA
    return pl.pallas_call(
        gather_kernel,
        out_shape=(
            jax.ShapeDtypeStruct((2, SIDE, SIDE), F32),
            jax.ShapeDtypeStruct((NP, NQ, 16, 128), jnp.int32),
        ),
        in_specs=[ANY, ANY],
        out_specs=(ANY, ANY),
        scratch_shapes=[dma, dma((NQ,)), dma((NQ,)), dma, dma((NQ + NP,)), dma((NQ + NP,))],
        compiler_params=pltpu.CompilerParams(collective_id=0, has_side_effects=True),
        name="gather_rows",
    )(spectra, gtile)


def spread_kernel(send, recv, own_sem, send_sem, recv_sem):
    p, q = lax.axis_index("freq"), lax.axis_index("rcv")
    me = p * NQ + q
    n = NP * NQ
    barrier = pltpu.get_barrier_semaphore()

    def greet(t, _):
        other = lax.rem(me + t, n)
        pl.semaphore_signal(barrier, inc=1, device_id=(other // NQ, lax.rem(other, NQ)), device_id_type=MESH)
        return 0

    lax.fori_loop(1, n, greet, 0)
    own = pltpu.make_async_copy(send.at[p, q], recv.at[me], own_sem)
    own.start()
    pl.semaphore_wait(barrier, n - 1)

    def put(t, _):
        other = lax.rem(me + t, n)
        pp, qq = other // NQ, lax.rem(other, NQ)
        pltpu.make_async_remote_copy(
            send.at[pp, qq], recv.at[me], send_sem, recv_sem, device_id=(pp, qq), device_id_type=MESH).start()
        return 0

    lax.fori_loop(1, n, put, 0)
    own.wait()
    most = recv.at[pl.ds(0, n - 1)]
    pltpu.make_async_copy(most, most, send_sem).wait()
    pltpu.make_async_copy(most, most, recv_sem).wait()


def spread(send):
    dma = pltpu.SemaphoreType.DMA
    return pl.pallas_call(
        spread_kernel,
        out_shape=jax.ShapeDtypeStruct((NP * NQ, 32, 128), F32),
        in_specs=[ANY],
        out_specs=ANY,
        scratch_shapes=[dma, dma, dma],
        compiler_params=pltpu.CompilerParams(collective_id=1, has_side_effects=True),
        name="spread",
    )(send)


def lane_group():
    return lax.broadcasted_iota(jnp.int32, (16, 128), 1) // 32


def swap_groups(blocks, group):
    outs = []
    for g in range(4):
        out = blocks[g]
        for u in range(4):
            if u != g:
                moved = pltpu.roll(blocks[u], (32 * (u - g)) % 128, 1)
                out = jnp.where(group == u, moved, out)
        outs.append(out)
    return outs


def nt(a, b):
    return lax.dot_general(a, b, (((1,), (1,)), ((), ())), preferred_element_type=F32)


def nn(a, b):
    return jnp.dot(a, b, preferred_element_type=F32)


def dot3(a, b):
    return nn(a[0], b[0]) + (nn(a[0], b[1]) + nn(a[1], b[0]))


def look_up(index, entries):
    level = entries
    for bit in range(4):
        odd = (index & (1 << bit)) != 0
        level = [jnp.where(odd, level[2 * k + 1], level[2 * k]) for k in range(len(level) // 2)]
    return level[0]


def products_kernel(whole, gains, prow, tab, send, d, ct, index, mirror, gain, mgain, direct, refl):
    group = lane_group()
    for b in range(2):
        rows = lax.broadcasted_iota(jnp.int32, (256, 256), 0) + 256 * b
        ct[b] = (rows == prow[:, 256 * b : 256 * b + 256]).astype(F32).T.astype(BF16)

    def place(p, _):
        for h in range(4):
            outs = swap_groups([gains[p, 4 * h + u] for u in range(4)], group)
            for g in range(4):
                index[pl.ds(pl.multiple_of(p * 64 + g * 16, 16), 16), 128 * h : 128 * h + 128] = outs[g]
        return 0

    lax.fori_loop(0, NP, place, 0)
    for a in range(2):
        for b in range(2):
            block = index[256 * b : 256 * b + 256, 256 * a : 256 * a + 256].astype(F32).astype(BF16)
            moved = nt(ct[a], block).astype(BF16)
            mirror[256 * a : 256 * a + 256, 256 * b : 256 * b + 256] = nn(moved, ct[b]).astype(jnp.int32)

    def gains_of(i, _):
        rows = pl.ds(pl.multiple_of(i * 16, 16), 16)
        for o in range(2):
            entries = [0.5 * tab[o, k] for k in range(16)]
            gain[o, rows, :] = look_up(index[rows, :], entries)
            mgain[o, rows, :] = look_up(mirror[rows, :], entries)
        return 0

    lax.fori_loop(0, SIDE // 16, gains_of, 0)

    def turn(i, _):
        rows = pl.ds(pl.multiple_of(i * 128, 128), 128)
        for h in range(4):
            cols = slice(128 * h, 128 * h + 128)
            real, imag = whole[0, rows, cols].T, whole[1, rows, cols].T
            for k, part in enumerate((real, imag, real + imag)):
                d[2 * k, cols, rows], d[2 * k + 1, cols, rows] = halves(part)
        return 0

    lax.fori_loop(0, 4, turn, 0)

    def multiply(left):
        one = dot3(left[0], (d[0], d[1]))
        two = dot3(left[1], (d[2], d[3]))
        three = dot3(left[2], (d[4], d[5]))
        return one - two, three - one - two

    def band(i, _):
        rows = pl.ds(pl.multiple_of(i * 256, 256), 256)
        first = multiply([(d[2 * k, rows, :], d[2 * k + 1, rows, :]) for k in range(3)])
        second = multiply([halves(x) for x in (first[0], first[1], first[0] + first[1])])
        for c in range(2):
            direct[c, rows, :] = gain[0, rows, :] * first[c] + gain[1, rows, :] * second[c]
            refl[2 * c, rows, :], refl[2 * c + 1, rows, :] = halves(
                mgain[0, rows, :] * first[c] + mgain[1, rows, :] * second[c])
        return 0

    lax.fori_loop(0, 2, band, 0)
    for a in range(2):
        for b in range(2):
            ra, rb = slice(256 * a, 256 * a + 256), slice(256 * b, 256 * b + 256)
            for c in range(2):
                high = nt(ct[a], refl[2 * c, rb, ra]).astype(BF16)
                low = nt(ct[a], refl[2 * c + 1, rb, ra]).astype(BF16)
                both = direct[c, ra, rb] + (nn(high, ct[b]) + nn(low, ct[b]))
                for i in range(4):
                    for h in range(2):
                        part = both[64 * i : 64 * i + 64, 128 * h : 128 * h + 128]
                        outs = swap_groups([part[16 * u : 16 * u + 16] for u in range(4)], group)
                        for u in range(4):
                            send[4 * a + i, 8 * b + 4 * h + u, 16 * c : 16 * c + 16, :] = outs[u]


def products(whole, gains, prow, tab):
    return pl.pallas_call(
        products_kernel,
        out_shape=jax.ShapeDtypeStruct((NP, NQ, 32, 128), F32),
        in_specs=[VMEM, VMEM, VMEM, SMEM],
        out_specs=VMEM,
        scratch_shapes=[
            pltpu.VMEM((6, SIDE, SIDE), BF16),
            pltpu.VMEM((2, 256, 256), BF16),
            pltpu.VMEM((SIDE, SIDE), jnp.int32),
            pltpu.VMEM((SIDE, SIDE), jnp.int32),
            pltpu.VMEM((2, SIDE, SIDE), F32),
            pltpu.VMEM((2, SIDE, SIDE), F32),
            pltpu.VMEM((2, SIDE, SIDE), F32),
            pltpu.VMEM((4, SIDE, SIDE), BF16),
        ],
        compiler_params=pltpu.CompilerParams(vmem_limit_bytes=56 << 20),
        name="products",
    )(whole, gains, prow, tab)


STEP = 2


def time_kernel(order, recv, table, recorded, out, held, sem):
    @pl.when(pl.program_id(0) == 0)
    def _():
        def fetch(l, _):
            pltpu.make_async_copy(recv.at[order[l]], held.at[pl.ds(l * 32, 32), :], sem).start()
            return 0

        lax.fori_loop(0, LIVE, fetch, 0)
        pltpu.make_async_copy(held, held, sem).wait()

    for k in range(STEP):
        j = pl.program_id(0) * STEP + k
        parts = [held[pl.ds(c * 16 + j, LIVE, stride=32), :] for c in range(2)]
        high, low = halves(jnp.concatenate(parts, axis=0).T)
        wave = nn(jnp.concatenate([high, low, high], axis=1), table[...])
        out[:, k] = recorded[:, k] - wave.reshape(4, 32, NT)


def to_time(order, recv, table, recorded):
    block = pl.BlockSpec((4, STEP, 32, NT), lambda j, order: (0, j, 0, 0))
    return pl.pallas_call(
        time_kernel,
        out_shape=jax.ShapeDtypeStruct((4, 16, 32, NT), F32),
        grid_spec=pltpu.PrefetchScalarGridSpec(
            num_scalar_prefetch=1,
            grid=(16 // STEP,),
            in_specs=[ANY, VMEM, block],
            out_specs=block,
            scratch_shapes=[pltpu.VMEM((LIVE * 32, 128), F32), pltpu.SemaphoreType.DMA],
        ),
        name="to_time",
    )(order, recv, table, recorded)


def on_device(spectra, counts, partner, recorded, gain_index, gain_table):
    gtile = gain_index.reshape(4, 16, 32).transpose(1, 0, 2).reshape(16, 128)
    live = jnp.arange(LIVE, dtype=jnp.int32)[:, None]
    order = live[:, 0] + jnp.sum(jnp.where(live >= jnp.cumsum(counts)[None, :], 16 - counts[None, :], 0), axis=1)
    whole, gains = gather_rows(spectra, gtile)
    send = products(whole, gains, partner.reshape(1, SIDE), gain_table)
    recv = spread(send)
    out = to_time(order.astype(jnp.int32), recv, jnp.asarray(basis()), recorded.reshape(4, 16, 32, NT))
    return out.reshape(64, 32, NT)


def solution(mesh):
    placed = (P("freq", None, "rcv", None), P(), P(), P("freq", "rcv", None), P("freq", "rcv"), P())
    return jax.shard_map(
        on_device, mesh=mesh, in_specs=placed, out_specs=P("freq", "rcv", None), check_vma=False
    )
```

```python
import itertools

import jax
import jax.numpy as jnp
import numpy as np
from jax import lax
from jax.experimental import pallas as pl
from jax.experimental.pallas import tpu as pltpu
from jax.sharding import PartitionSpec as P

MESH = pl.DeviceIdType.MESH
ANY = pl.BlockSpec(memory_space=pl.ANY)
VMEM = pl.BlockSpec(memory_space=pltpu.VMEM)
SMEM = pl.BlockSpec(memory_space=pltpu.SMEM)

NT = 512
SIDE = 512
LIVE = 64
NP = 8
NQ = 16
F32 = jnp.float32
BF16 = jnp.bfloat16


def basis():
    bins = np.arange(1, LIVE + 1, dtype=np.int64)[:, None]
    angles = 2.0 * np.pi / NT * ((bins * np.arange(NT, dtype=np.int64)[None, :]) % NT)
    table = np.concatenate([np.cos(angles), -np.sin(angles)], axis=0).astype(np.float32)
    high = table.astype(BF16)
    low = (table - high.astype(np.float32)).astype(BF16)
    return np.concatenate([high, high, low], axis=0)


def halves(x):
    high = x.astype(BF16)
    return high, (x - high.astype(F32)).astype(BF16)


def lane_group():
    return lax.broadcasted_iota(jnp.int32, (16, 128), 1) // 32


def swap_groups(blocks, group):
    outs = []
    for g in range(4):
        out = blocks[g]
        for u in range(4):
            if u != g:
                moved = pltpu.roll(blocks[u], (32 * (u - g)) % 128, 1)
                out = jnp.where(group == u, moved, out)
        outs.append(out)
    return outs


def nt(a, b):
    return lax.dot_general(a, b, (((1,), (1,)), ((), ())), preferred_element_type=F32)


def nn(a, b):
    return jnp.dot(a, b, preferred_element_type=F32)


def look_up(index, entries):
    level = entries
    for bit in range(4):
        odd = (index & (1 << bit)) != 0
        level = [jnp.where(odd, level[2 * k + 1], level[2 * k]) for k in range(len(level) // 2)]
    return level[0]


def each(first, last, fn):
    def body(t, _):
        fn(t)
        return 0

    lax.fori_loop(first, last, body, 0)


def away(a, code):
    return a + code * (4 - 2 * a)


def ways(a):
    return 2 if a == 1 else 1


def far_first(ranges):
    return sorted(itertools.product(range(3), repeat=ranges), key=lambda c: (-sum(c), c))


def slot_kernel(
    spec, gtile, prow, tab, recv,
    whole, gains, ct, index, mirror, gain, mgain, d, direct, refl, both, send,
    own_sem, row_send, row_recv, tile_send, tile_recv, slab_send, slab_recv, turn_sem, ready_sem,
    out_own, out_send, out_recv,
):
    p, q = lax.axis_index("freq"), lax.axis_index("rcv")
    me = p * NQ + q
    z, core = p // 2, lax.rem(p, 2)
    x, y = q // 4, lax.rem(q, 4)
    mate = p + 1 - 2 * core

    barrier = pltpu.get_barrier_semaphore()

    def greet_q(t):
        pl.semaphore_signal(barrier, inc=1, device_id=(p, lax.rem(q + t, NQ)), device_id_type=MESH)

    def greet_p(t):
        pl.semaphore_signal(barrier, inc=1, device_id=(lax.rem(p + t, NP), q), device_id_type=MESH)

    each(1, NQ, greet_q)
    each(1, NP, greet_p)
    own_tile = pltpu.make_async_copy(gtile, gains.at[p, q], own_sem.at[0])
    own_rows = pltpu.make_async_copy(spec.at[q], whole.at[:, pl.ds(pl.multiple_of(q * 32, 32), 32), :], own_sem.at[1])
    own_tile.start()
    own_rows.start()
    for b in range(2):
        rows = lax.broadcasted_iota(jnp.int32, (256, 256), 0) + 256 * b
        ct[b] = (rows == prow[:, 256 * b : 256 * b + 256]).astype(F32).T.astype(BF16)
    pl.semaphore_wait(barrier, NQ + NP - 2)
    each(1, NP, lambda t: pl.semaphore_signal(
        ready_sem, inc=1, device_id=(lax.rem(p + t, NP), q), device_id_type=MESH))

    def tile(t):
        return pltpu.make_async_remote_copy(
            gtile, gains.at[p, q], tile_send.at[t], tile_recv.at[t],
            device_id=(p, lax.rem(q + t, NQ)), device_id_type=MESH)

    def row(t):
        k = lax.rem(q + t, NQ)
        return pltpu.make_async_remote_copy(
            spec.at[k], whole.at[:, pl.ds(pl.multiple_of(q * 32, 32), 32), :], row_send.at[t], row_recv.at[t],
            device_id=(p, k), device_id_type=MESH)

    def slab(k, target, t):
        return pltpu.make_async_remote_copy(
            gains.at[k], gains.at[k], slab_send.at[t], slab_recv.at[k],
            device_id=(target, q), device_id_type=MESH)

    each(1, NQ, lambda t: tile(t).start())

    @pl.when(core == 0)
    def _():
        each(1, NQ, lambda t: row(t).start())

    own_tile.wait()
    each(1, NQ, lambda t: tile(t).wait())

    each(1, 4, lambda t: slab(p, lax.rem(z + t, 4) * 2, t).start())

    @pl.when(core == 1)
    def _():
        slab(p, p - 1, 0).start()

    @pl.when(core == 0)
    def _():
        each(1, NP, lambda t: slab(lax.rem(p + t, NP), 0, 0).wait_recv())
        each(1, NP, lambda t: slab(lax.rem(p + 1 + t, NP), p + 1, t + 3).start())
        each(1, NQ, lambda t: row(t).wait_send())
        pl.semaphore_signal(turn_sem, inc=1, device_id=(p + 1, q), device_id_type=MESH)

    @pl.when(core == 1)
    def _():
        pl.semaphore_wait(turn_sem, 1)
        each(1, NQ, lambda t: row(t).start())
        each(1, NP, lambda t: slab(lax.rem(p + t, NP), 0, 0).wait_recv())

    group = lane_group()

    def place(k):
        for h in range(4):
            outs = swap_groups([gains[k, 4 * h + u] for u in range(4)], group)
            for g in range(4):
                index[h, pl.ds(k * 64 + g, 16, stride=4), :] = outs[g]

    each(0, NP, place)
    for a in range(2):
        for b in range(2):
            block = jnp.concatenate([index[2 * a + h, 256 * b : 256 * b + 256, :] for h in range(2)], axis=1).astype(F32).astype(BF16)
            moved = nt(ct[a], block).astype(BF16)
            mirror[256 * a : 256 * a + 256, 256 * b : 256 * b + 256] = nn(moved, ct[b]).astype(jnp.int32)

    def gains_of(i):
        rows = pl.ds(pl.multiple_of(i * 16, 16), 16)
        for o in range(2):
            entries = [0.5 * tab[o, k] for k in range(16)]
            for h in range(4):
                gain[o, rows, 128 * h : 128 * h + 128] = look_up(index[h, rows, :], entries)
            mgain[o, rows, :] = look_up(mirror[rows, :], entries)

    each(0, SIDE // 16, gains_of)
    own_rows.wait()
    each(1, NQ, lambda t: row(t).wait_recv())

    @pl.when(core == 1)
    def _():
        each(1, NQ, lambda t: row(t).wait_send())

    def turn(i):
        rows = pl.ds(pl.multiple_of(i * 128, 128), 128)
        for h in range(4):
            at = 128 * h
            real, imag = whole[0, rows, at : at + 128].T, whole[1, rows, at : at + 128].T
            for k, part in enumerate((real, imag, real + imag)):
                high, low = halves(part)
                d[k, at : at + 128, rows] = high
                d[k, SIDE + at : SIDE + at + 128, rows] = low
                d[k, 2 * SIDE + at : 2 * SIDE + at + 128, rows] = high

    each(0, 4, turn)

    def multiply(left):
        one, two, three = (
            nn(jnp.concatenate([high, high, low], axis=1), d[k]) for k, (high, low) in enumerate(left))
        return one - two, three - one - two

    def band(i):
        rows = pl.ds(pl.multiple_of(i * BAND, BAND), BAND)
        lows = pl.ds(pl.multiple_of(SIDE + i * BAND, BAND), BAND)
        first = multiply([(d[k, rows, :], d[k, lows, :]) for k in range(3)])
        second = multiply([halves(v) for v in (first[0], first[1], first[0] + first[1])])
        for c in range(2):
            direct[c, rows, :] = gain[0, rows, :] * first[c] + gain[1, rows, :] * second[c]
            refl[2 * c, rows, :], refl[2 * c + 1, rows, :] = halves(
                mgain[0, rows, :] * first[c] + mgain[1, rows, :] * second[c])

    each(0, SIDE // BAND, band)
    for a in range(2):
        for b in range(2):
            ra, rb = slice(256 * a, 256 * a + 256), slice(256 * b, 256 * b + 256)
            for c in range(2):
                high = nt(ct[a], refl[2 * c, rb, ra]).astype(BF16)
                low = nt(ct[a], refl[2 * c + 1, rb, ra]).astype(BF16)
                total = direct[c, ra, rb] + (nn(high, ct[b]) + nn(low, ct[b]))
                for h in range(2):
                    both[c, h] = total[:, 128 * h : 128 * h + 128]

            def pack(i):
                for c in range(2):
                    for h in range(2):
                        outs = swap_groups(
                            [both[c, h, pl.ds(i * 64 + u, 16, stride=4), :] for u in range(4)], group)
                        for u in range(4):
                            send[4 * a + i, 8 * b + 4 * h + u, 16 * c : 16 * c + 16, :] = outs[u]

            each(0, 4, pack)

    pl.semaphore_wait(ready_sem, NP - 1)
    mine = pltpu.make_async_copy(send.at[p, q], recv.at[me], out_own)
    mine.start()
    for a, b, c in far_first(3):
        def put(e):
            dc, e = lax.rem(e, 2), e // 2
            dx, e = away(a, lax.rem(e, ways(a))), e // ways(a)
            dy, e = away(b, lax.rem(e, ways(b))), e // ways(b)
            dz = away(c, e)
            pp = lax.rem(z + dz, 4) * 2 + lax.rem(core + dc, 2)
            qq = lax.rem(x + dx, 4) * 4 + lax.rem(y + dy, 4)
            pltpu.make_async_remote_copy(
                send.at[pp, qq], recv.at[me], out_send, out_recv, device_id=(pp, qq), device_id_type=MESH).start()

        each(1 if a + b + c == 0 else 0, 2 * ways(a) * ways(b) * ways(c), put)
    each(1, 4, lambda t: slab(p, 0, t).wait_send())

    @pl.when(core == 1)
    def _():
        slab(p, 0, 0).wait_send()

    @pl.when(core == 0)
    def _():
        each(1, NP, lambda t: slab(0, 0, t + 3).wait_send())

    mine.wait()
    most = recv.at[pl.ds(0, NP * NQ - 1)]
    pltpu.make_async_copy(most, most, out_send).wait()
    pltpu.make_async_copy(most, most, out_recv).wait()


BAND = 256


def slot_work(spectra, gtile, prow, tab):
    dma = pltpu.SemaphoreType.DMA
    regular = pltpu.SemaphoreType.REGULAR
    return pl.pallas_call(
        slot_kernel,
        out_shape=jax.ShapeDtypeStruct((NP * NQ, 32, 128), F32),
        in_specs=[ANY, VMEM, VMEM, SMEM],
        out_specs=ANY,
        scratch_shapes=[
            pltpu.VMEM((2, SIDE, SIDE), F32),
            pltpu.VMEM((NP, NQ, 16, 128), jnp.int32),
            pltpu.VMEM((2, 256, 256), BF16),
            pltpu.VMEM((4, SIDE, 128), jnp.int32),
            pltpu.VMEM((SIDE, SIDE), jnp.int32),
            pltpu.VMEM((2, SIDE, SIDE), F32),
            pltpu.VMEM((2, SIDE, SIDE), F32),
            pltpu.VMEM((3, 3 * SIDE, SIDE), BF16),
            pltpu.VMEM((2, SIDE, SIDE), F32),
            pltpu.VMEM((4, SIDE, SIDE), BF16),
            pltpu.VMEM((2, 2, 256, 128), F32),
            pltpu.VMEM((NP, NQ, 32, 128), F32),
            dma((2,)), dma((NQ,)), dma((NQ,)), dma((NQ,)), dma((NQ,)), dma((11,)), dma((NP,)), regular, regular,
            dma, dma, dma,
        ],
        compiler_params=pltpu.CompilerParams(
            collective_id=0, has_side_effects=True, vmem_limit_bytes=48 << 20),
        name="slot_work",
    )(spectra, gtile, prow, tab)


PART = 8


def time_kernel(counts, recv, table, recorded, out, held, rec, res, fetch_sem, in_sem, out_sem):
    def load(i):
        at = pl.ds(i * PART, PART)
        return pltpu.make_async_copy(recorded.at[at], rec.at[at], in_sem.at[i])

    def store(i):
        at = pl.ds(i * PART, PART)
        return pltpu.make_async_copy(res.at[at], out.at[at], out_sem.at[i])

    parts = 64 // PART
    row = 0
    for p in range(NP):
        live = counts[p]

        def fetch(k):
            pltpu.make_async_copy(
                recv.at[p * NQ + k], held.at[pl.ds(pl.multiple_of((row + k) * 32, 32), 32), :], fetch_sem).start()

        each(0, live, fetch)
        row = row + live
    each(0, parts, lambda i: load(i).start())
    pltpu.make_async_copy(held, held, fetch_sem).wait()

    def part(i):
        load(i).wait()
        for k in range(PART // 4):
            j = i * (PART // 4) + k
            values = [held[pl.ds(c * 16 + j, LIVE, stride=32), :] for c in range(2)]
            high, low = halves(jnp.concatenate(values, axis=0).T)
            wave = nn(jnp.concatenate([high, low, high], axis=1), table[...])
            at = pl.ds(pl.multiple_of(4 * j, 4), 4)
            res[at] = rec[at] - wave.reshape(4, 32, NT)
        store(i).start()

    each(0, parts, part)
    each(0, parts, lambda i: store(i).wait())


def to_time(counts, recv, table, recorded):
    dma = pltpu.SemaphoreType.DMA
    return pl.pallas_call(
        time_kernel,
        out_shape=jax.ShapeDtypeStruct((64, 32, NT), F32),
        in_specs=[SMEM, ANY, VMEM, ANY],
        out_specs=ANY,
        scratch_shapes=[
            pltpu.VMEM((LIVE * 32, 128), F32),
            pltpu.VMEM((64, 32, NT), F32),
            pltpu.VMEM((64, 32, NT), F32),
            dma, dma((64 // PART,)), dma((64 // PART,)),
        ],
        name="to_time",
    )(counts, recv, table, recorded)


def on_device(spectra, counts, partner, recorded, gain_index, gain_table):
    gtile = gain_index.reshape(16, 128)
    recv = slot_work(spectra, gtile, partner.reshape(1, SIDE), gain_table)
    return to_time(counts, recv, jnp.asarray(basis()), recorded)


def solution(mesh):
    placed = (P("freq", None, "rcv", None), P(), P(), P("freq", "rcv", None), P("freq", "rcv"), P())
    return jax.shard_map(
        on_device, mesh=mesh, in_specs=placed, out_specs=P("freq", "rcv", None), check_vma=False
    )
```

```python
import itertools
import random

import jax
import jax.numpy as jnp
import numpy as np
from jax import lax
from jax.experimental import pallas as pl
from jax.experimental.pallas import tpu as pltpu
from jax.sharding import PartitionSpec as P

MESH = pl.DeviceIdType.MESH
ANY = pl.BlockSpec(memory_space=pl.ANY)
VMEM = pl.BlockSpec(memory_space=pltpu.VMEM)
SMEM = pl.BlockSpec(memory_space=pltpu.SMEM)

NT = 512
SIDE = 512
LIVE = 64
NP = 8
NQ = 16
F32 = jnp.float32
BF16 = jnp.bfloat16


def basis():
    bins = np.arange(1, LIVE + 1, dtype=np.int64)[:, None]
    angles = 2.0 * np.pi / NT * ((bins * np.arange(NT, dtype=np.int64)[None, :]) % NT)
    table = np.concatenate([np.cos(angles), -np.sin(angles)], axis=0).astype(np.float32)
    high = table.astype(BF16)
    low = (table - high.astype(np.float32)).astype(BF16)
    return np.concatenate([high, high, low], axis=0)


def halves(x):
    high = x.astype(BF16)
    return high, (x - high.astype(F32)).astype(BF16)


def lane_group():
    return lax.broadcasted_iota(jnp.int32, (16, 128), 1) // 32


def swap_groups(blocks, group):
    outs = []
    for g in range(4):
        out = blocks[g]
        for u in range(4):
            if u != g:
                moved = pltpu.roll(blocks[u], (32 * (u - g)) % 128, 1)
                out = jnp.where(group == u, moved, out)
        outs.append(out)
    return outs


def nt(a, b):
    return lax.dot_general(a, b, (((1,), (1,)), ((), ())), preferred_element_type=F32)


def nn(a, b):
    return jnp.dot(a, b, preferred_element_type=F32)


def look_up(index, entries):
    level = entries
    for bit in range(4):
        odd = (index & (1 << bit)) != 0
        level = [jnp.where(odd, level[2 * k + 1], level[2 * k]) for k in range(len(level) // 2)]
    return level[0]


def each(first, last, fn):
    def body(t, _):
        fn(t)
        return 0

    lax.fori_loop(first, last, body, 0)


def near(offset):
    return sum(min(step, 4 - step) for step in offset[:3])


def far_first(shape, seed):
    offsets = [offset for offset in itertools.product(*map(range, shape)) if any(offset)]
    random.Random(seed).shuffle(offsets)
    return sorted(offsets, key=lambda offset: -near(offset))


def slot_kernel(
    spec, gindex, partner, table, recv,
    gtile, prow, tab, whole, gains, ct, index, mirror, gain, mgain, d, direct, refl, both, send,
    own_sem, row_send, row_recv, tile_send, tile_recv, slab_send, slab_recv, turn_sem, ready_sem,
    out_own, out_send, out_recv,
):
    p, q = lax.axis_index("freq"), lax.axis_index("rcv")
    me = p * NQ + q
    z, core = p // 2, lax.rem(p, 2)
    x, y = q // 4, lax.rem(q, 4)
    mate = p + 1 - 2 * core

    barrier = pltpu.get_barrier_semaphore()

    def greet_q(t):
        pl.semaphore_signal(barrier, inc=1, device_id=(p, lax.rem(q + t, NQ)), device_id_type=MESH)

    def greet_p(t):
        pl.semaphore_signal(barrier, inc=1, device_id=(lax.rem(p + t, NP), q), device_id_type=MESH)

    each(1, NQ, greet_q)
    each(1, NP, greet_p)
    small = [pltpu.make_async_copy(src, dst, own_sem.at[i + 1]) for i, (src, dst) in enumerate(
        ((gindex, gtile), (partner, prow), (table, tab)))]
    for copy in small:
        copy.start()
    own_rows = pltpu.make_async_copy(spec.at[q], whole.at[:, pl.ds(pl.multiple_of(q * 32, 32), 32), :], own_sem.at[0])
    own_rows.start()
    small[0].wait()
    lanes = lax.broadcasted_iota(jnp.int32, (128, 32), 0)
    repeat = (lax.rem(lanes, 32) == lax.broadcasted_iota(jnp.int32, (128, 32), 1)).astype(BF16)
    levels = nn(repeat, gtile[...].astype(F32).astype(BF16))
    sources = lax.broadcasted_iota(jnp.int32, (128, 64), 1)
    groups = lax.broadcasted_iota(jnp.int32, (128, 64), 0) // 32
    levels = jnp.where(lax.rem(sources, 4) == groups, levels, 0.0).astype(BF16)
    fours = lax.broadcasted_iota(jnp.int32, (16, 64), 1) // 4
    fours = (fours == lax.broadcasted_iota(jnp.int32, (16, 64), 0)).astype(BF16)
    gains[p, q] = nt(fours, levels).astype(jnp.int32)
    small[1].wait()
    small[2].wait()
    for b in range(2):
        rows = lax.broadcasted_iota(jnp.int32, (256, 256), 0) + 256 * b
        ct[b] = (rows == prow[:, 256 * b : 256 * b + 256]).astype(F32).T.astype(BF16)
    pl.semaphore_wait(barrier, NQ + NP - 2)
    each(1, NP, lambda t: pl.semaphore_signal(
        ready_sem, inc=1, device_id=(lax.rem(p + t, NP), q), device_id_type=MESH))

    def at_offset(dx, dy):
        return lax.rem(x + dx, 4) * 4 + lax.rem(y + dy, 4)

    def tile(t):
        return pltpu.make_async_remote_copy(
            gains.at[p, q], gains.at[p, q], tile_send.at[t], tile_recv.at[t],
            device_id=(p, at_offset(t // 4, lax.rem(t, 4))), device_id_type=MESH)

    def row(t):
        k = at_offset(t // 4, lax.rem(t, 4))
        return pltpu.make_async_remote_copy(
            spec.at[k], whole.at[:, pl.ds(pl.multiple_of(q * 32, 32), 32), :], row_send.at[t], row_recv.at[t],
            device_id=(p, k), device_id_type=MESH)

    def slab(k, target, t):
        return pltpu.make_async_remote_copy(
            gains.at[k], gains.at[k], slab_send.at[t], slab_recv.at[k],
            device_id=(target, q), device_id_type=MESH)

    each(1, NQ, lambda t: tile(t).start())

    def start_rows():
        for dx, dy in far_first((4, 4), 0):
            row(4 * dx + dy).start()

    @pl.when(core == 0)
    def _():
        start_rows()

    each(1, NQ, lambda t: tile(t).wait())

    each(1, 4, lambda t: slab(p, lax.rem(z + t, 4) * 2, t).start())

    @pl.when(core == 1)
    def _():
        slab(p, p - 1, 0).start()

    @pl.when(core == 0)
    def _():
        each(1, NP, lambda t: slab(lax.rem(p + t, NP), 0, 0).wait_recv())
        each(1, NP, lambda t: slab(lax.rem(p + 1 + t, NP), p + 1, t + 3).start())
        each(1, NQ, lambda t: row(t).wait_send())
        pl.semaphore_signal(turn_sem, inc=1, device_id=(p + 1, q), device_id_type=MESH)

    @pl.when(core == 1)
    def _():
        pl.semaphore_wait(turn_sem, 1)
        start_rows()
        each(1, NP, lambda t: slab(lax.rem(p + t, NP), 0, 0).wait_recv())

    group = lane_group()

    def place(k):
        for h in range(4):
            outs = swap_groups([gains[k, 4 * h + u] for u in range(4)], group)
            for g in range(4):
                index[h, pl.ds(k * 64 + g, 16, stride=4), :] = outs[g]

    each(0, NP, place)
    for a in range(2):
        for b in range(2):
            block = jnp.concatenate([index[2 * a + h, 256 * b : 256 * b + 256, :] for h in range(2)], axis=1).astype(F32).astype(BF16)
            moved = nt(ct[a], block).astype(BF16)
            mirror[256 * a : 256 * a + 256, 256 * b : 256 * b + 256] = nn(moved, ct[b]).astype(jnp.int32)

    def gains_of(i):
        rows = pl.ds(pl.multiple_of(i * 16, 16), 16)
        for o in range(2):
            entries = [0.5 * tab[o, k] for k in range(16)]
            for h in range(4):
                gain[o, rows, 128 * h : 128 * h + 128] = look_up(index[h, rows, :], entries)
            mgain[o, rows, :] = look_up(mirror[rows, :], entries)

    each(0, SIDE // 16, gains_of)
    own_rows.wait()
    each(1, NQ, lambda t: row(t).wait_recv())

    @pl.when(core == 1)
    def _():
        each(1, NQ, lambda t: row(t).wait_send())

    def turn(i):
        rows = pl.ds(pl.multiple_of(i * 128, 128), 128)
        for h in range(4):
            at = 128 * h
            real, imag = whole[0, rows, at : at + 128].T, whole[1, rows, at : at + 128].T
            for k, part in enumerate((real, imag, real + imag)):
                high, low = halves(part)
                d[k, at : at + 128, rows] = high
                d[k, SIDE + at : SIDE + at + 128, rows] = low
                d[k, 2 * SIDE + at : 2 * SIDE + at + 128, rows] = high

    each(0, 4, turn)

    def multiply(left):
        one, two, three = (
            nn(jnp.concatenate([high, high, low], axis=1), d[k]) for k, (high, low) in enumerate(left))
        return one - two, three - one - two

    def band(i):
        rows = pl.ds(pl.multiple_of(i * BAND, BAND), BAND)
        lows = pl.ds(pl.multiple_of(SIDE + i * BAND, BAND), BAND)
        first = multiply([(d[k, rows, :], d[k, lows, :]) for k in range(3)])
        second = multiply([halves(v) for v in (first[0], first[1], first[0] + first[1])])
        for c in range(2):
            direct[c, rows, :] = gain[0, rows, :] * first[c] + gain[1, rows, :] * second[c]
            refl[2 * c, rows, :], refl[2 * c + 1, rows, :] = halves(
                mgain[0, rows, :] * first[c] + mgain[1, rows, :] * second[c])

    each(0, SIDE // BAND, band)
    for a in range(2):
        for b in range(2):
            ra, rb = slice(256 * a, 256 * a + 256), slice(256 * b, 256 * b + 256)
            for c in range(2):
                high = nt(ct[a], refl[2 * c, rb, ra]).astype(BF16)
                low = nt(ct[a], refl[2 * c + 1, rb, ra]).astype(BF16)
                total = direct[c, ra, rb] + (nn(high, ct[b]) + nn(low, ct[b]))
                for h in range(2):
                    both[c, h] = total[:, 128 * h : 128 * h + 128]

            def pack(i):
                for c in range(2):
                    for h in range(2):
                        outs = swap_groups(
                            [both[c, h, pl.ds(i * 64 + u, 16, stride=4), :] for u in range(4)], group)
                        for u in range(4):
                            send[4 * a + i, 8 * b + 4 * h + u, 16 * c : 16 * c + 16, :] = outs[u]

            each(0, 4, pack)

    pl.semaphore_wait(ready_sem, NP - 1)
    mine = pltpu.make_async_copy(send.at[p, q], recv.at[me], out_own)
    mine.start()
    for dx, dy, dz, dc in far_first((4, 4, 4, 2), 2):
        pp = lax.rem(z + dz, 4) * 2 + lax.rem(core + dc, 2)
        qq = at_offset(dx, dy)
        pltpu.make_async_remote_copy(
            send.at[pp, qq], recv.at[me], out_send, out_recv, device_id=(pp, qq), device_id_type=MESH).start()
    each(1, 4, lambda t: slab(p, 0, t).wait_send())

    @pl.when(core == 1)
    def _():
        slab(p, 0, 0).wait_send()

    @pl.when(core == 0)
    def _():
        each(1, NP, lambda t: slab(0, 0, t + 3).wait_send())

    mine.wait()
    most = recv.at[pl.ds(0, NP * NQ - 1)]
    pltpu.make_async_copy(most, most, out_send).wait()
    pltpu.make_async_copy(most, most, out_recv).wait()


BAND = 256
K1_VMEM = 63 << 20


def slot_work(spectra, gindex, partner, table):
    dma = pltpu.SemaphoreType.DMA
    regular = pltpu.SemaphoreType.REGULAR
    return pl.pallas_call(
        slot_kernel,
        out_shape=jax.ShapeDtypeStruct((NP * NQ, 32, 128), F32),
        in_specs=[ANY, ANY, ANY, ANY],
        out_specs=ANY,
        scratch_shapes=[
            pltpu.VMEM((32, 64), jnp.int32),
            pltpu.VMEM((1, SIDE), jnp.int32),
            pltpu.SMEM((2, 16), F32),
            pltpu.VMEM((2, SIDE, SIDE), F32),
            pltpu.VMEM((NP, NQ, 16, 128), jnp.int32),
            pltpu.VMEM((2, 256, 256), BF16),
            pltpu.VMEM((4, SIDE, 128), jnp.int32),
            pltpu.VMEM((SIDE, SIDE), jnp.int32),
            pltpu.VMEM((2, SIDE, SIDE), F32),
            pltpu.VMEM((2, SIDE, SIDE), F32),
            pltpu.VMEM((3, 3 * SIDE, SIDE), BF16),
            pltpu.VMEM((2, SIDE, SIDE), F32),
            pltpu.VMEM((4, SIDE, SIDE), BF16),
            pltpu.VMEM((2, 2, 256, 128), F32),
            pltpu.VMEM((NP, NQ, 32, 128), F32),
            dma((4,)), dma((NQ,)), dma((NQ,)), dma((NQ,)), dma((NQ,)), dma((11,)), dma((NP,)), regular, regular,
            dma, dma, dma,
        ],
        compiler_params=pltpu.CompilerParams(
            collective_id=0, has_side_effects=True, vmem_limit_bytes=K1_VMEM),
        name="slot_work",
    )(spectra, gindex, partner, table)


PART = 8


def time_kernel(counts, recv, table, recorded, out, held, rec, res, fetch_sem, in_sem, out_sem):
    def load(i):
        at = pl.ds(i * PART, PART)
        return pltpu.make_async_copy(recorded.at[at], rec.at[at], in_sem.at[i])

    def store(i):
        at = pl.ds(i * PART, PART)
        return pltpu.make_async_copy(res.at[at], out.at[at], out_sem.at[i])

    parts = 64 // PART
    row = 0
    for p in range(NP):
        live = counts[p]

        def fetch(k):
            pltpu.make_async_copy(
                recv.at[p * NQ + k], held.at[pl.ds(pl.multiple_of((row + k) * 32, 32), 32), :], fetch_sem).start()

        each(0, live, fetch)
        row = row + live
    each(0, parts, lambda i: load(i).start())
    pltpu.make_async_copy(held, held, fetch_sem).wait()

    def part(i):
        load(i).wait()
        for k in range(PART // 4):
            j = i * (PART // 4) + k
            values = [held[pl.ds(c * 16 + j, LIVE, stride=32), :] for c in range(2)]
            high, low = halves(jnp.concatenate(values, axis=0).T)
            wave = nn(jnp.concatenate([high, low, high], axis=1), table[...])
            at = pl.ds(pl.multiple_of(4 * j, 4), 4)
            res[at] = rec[at] - wave.reshape(4, 32, NT)
        store(i).start()

    each(0, parts, part)
    each(0, parts, lambda i: store(i).wait())


def to_time(counts, recv, table, recorded):
    dma = pltpu.SemaphoreType.DMA
    return pl.pallas_call(
        time_kernel,
        out_shape=jax.ShapeDtypeStruct((64, 32, NT), F32),
        in_specs=[SMEM, ANY, VMEM, ANY],
        out_specs=ANY,
        scratch_shapes=[
            pltpu.VMEM((LIVE * 32, 128), F32),
            pltpu.VMEM((64, 32, NT), F32),
            pltpu.VMEM((64, 32, NT), F32),
            dma, dma((64 // PART,)), dma((64 // PART,)),
        ],
        name="to_time",
    )(counts, recv, table, recorded)


def on_device(spectra, counts, partner, recorded, gain_index, gain_table):
    recv = slot_work(spectra, gain_index.T, partner.reshape(1, SIDE), gain_table)
    return to_time(counts, recv, jnp.asarray(basis()), recorded)


def solution(mesh):
    placed = (P("freq", None, "rcv", None), P(), P(), P("freq", "rcv", None), P("freq", "rcv"), P())
    return jax.shard_map(
        on_device, mesh=mesh, in_specs=placed, out_specs=P("freq", "rcv", None), check_vma=False
    )
```

```python
import itertools
import random

import jax
import jax.numpy as jnp
import numpy as np
from jax import lax
from jax.experimental import pallas as pl
from jax.experimental.pallas import tpu as pltpu
from jax.sharding import PartitionSpec as P

MESH = pl.DeviceIdType.MESH
ANY = pl.BlockSpec(memory_space=pl.ANY)
VMEM = pl.BlockSpec(memory_space=pltpu.VMEM)
SMEM = pl.BlockSpec(memory_space=pltpu.SMEM)

NT = 512
SIDE = 512
LIVE = 64
NP = 8
NQ = 16
F32 = jnp.float32
BF16 = jnp.bfloat16


def basis():
    bins = np.arange(1, LIVE + 1, dtype=np.int64)[:, None]
    angles = 2.0 * np.pi / NT * ((bins * np.arange(NT, dtype=np.int64)[None, :]) % NT)
    table = np.concatenate([np.cos(angles), -np.sin(angles)], axis=0).astype(np.float32)
    high = table.astype(BF16)
    low = (table - high.astype(np.float32)).astype(BF16)
    return np.concatenate([high, high, low], axis=0)


def halves(x):
    high = x.astype(BF16)
    return high, (x - high.astype(F32)).astype(BF16)


def lane_group():
    return lax.broadcasted_iota(jnp.int32, (16, 128), 1) // 32


def swap_groups(blocks, group):
    for step in (2, 1):
        upper = (group & step) != 0
        swapped = list(blocks)
        for i in range(4):
            if not i & step:
                low, high = blocks[i], blocks[i + step]
                swapped[i] = jnp.where(upper, pltpu.roll(high, 32 * step, 1), low)
                swapped[i + step] = jnp.where(upper, high, pltpu.roll(low, 128 - 32 * step, 1))
        blocks = swapped
    return blocks


def nt(a, b):
    return lax.dot_general(a, b, (((1,), (1,)), ((), ())), preferred_element_type=F32)


def nn(a, b):
    return jnp.dot(a, b, preferred_element_type=F32)


def look_up(index, entries):
    level = entries
    for bit in range(4):
        odd = (index & (1 << bit)) != 0
        level = [jnp.where(odd, level[2 * k + 1], level[2 * k]) for k in range(len(level) // 2)]
    return level[0]


def each(first, last, fn):
    def body(t, _):
        fn(t)
        return 0

    lax.fori_loop(first, last, body, 0)


def near(offset):
    return sum(min(step, 4 - step) for step in offset[:3])


def far_first(shape, seed):
    offsets = [offset for offset in itertools.product(*map(range, shape)) if any(offset)]
    random.Random(seed).shuffle(offsets)
    return sorted(offsets, key=lambda offset: -near(offset))


def slot_kernel(
    spec, gindex, partner, table, recv,
    gtile, prow, tab, whole, gains, ct, index, mirror, gain, mgain, d, direct, refl, both, send,
    own_sem, row_send, row_recv, tile_send, tile_recv, slab_send, slab_recv, turn_sem, ready_sem,
    out_own, out_send, out_recv,
):
    p, q = lax.axis_index("freq"), lax.axis_index("rcv")
    me = p * NQ + q
    z, core = p // 2, lax.rem(p, 2)
    x, y = q // 4, lax.rem(q, 4)
    mate = p + 1 - 2 * core

    barrier = pltpu.get_barrier_semaphore()

    def greet_q(t):
        pl.semaphore_signal(barrier, inc=1, device_id=(p, lax.rem(q + t, NQ)), device_id_type=MESH)

    def greet_p(t):
        pl.semaphore_signal(barrier, inc=1, device_id=(lax.rem(p + t, NP), q), device_id_type=MESH)

    each(1, NQ, greet_q)
    each(1, NP, greet_p)
    small = [pltpu.make_async_copy(src, dst, own_sem.at[i + 1]) for i, (src, dst) in enumerate(
        ((gindex, gtile), (partner, prow), (table, tab)))]
    for copy in small:
        copy.start()
    own_rows = pltpu.make_async_copy(spec.at[q], whole.at[:, pl.ds(pl.multiple_of(q * 32, 32), 32), :], own_sem.at[0])
    own_rows.start()
    small[0].wait()
    lanes = lax.broadcasted_iota(jnp.int32, (128, 32), 0)
    repeat = (lax.rem(lanes, 32) == lax.broadcasted_iota(jnp.int32, (128, 32), 1)).astype(BF16)
    levels = nn(repeat, gtile[...].astype(F32).astype(BF16))
    sources = lax.broadcasted_iota(jnp.int32, (128, 64), 1)
    groups = lax.broadcasted_iota(jnp.int32, (128, 64), 0) // 32
    levels = jnp.where(lax.rem(sources, 4) == groups, levels, 0.0).astype(BF16)
    fours = lax.broadcasted_iota(jnp.int32, (16, 64), 1) // 4
    fours = (fours == lax.broadcasted_iota(jnp.int32, (16, 64), 0)).astype(BF16)
    gains[p, q] = nt(fours, levels).astype(jnp.int32)
    small[1].wait()
    small[2].wait()
    for b in range(2):
        rows = lax.broadcasted_iota(jnp.int32, (256, 256), 0) + 256 * b
        ct[b] = (rows == prow[:, 256 * b : 256 * b + 256]).astype(F32).T.astype(BF16)
    pl.semaphore_wait(barrier, NQ + NP - 2)
    each(1, NP, lambda t: pl.semaphore_signal(
        ready_sem, inc=1, device_id=(lax.rem(p + t, NP), q), device_id_type=MESH))

    def at_offset(dx, dy):
        return lax.rem(x + dx, 4) * 4 + lax.rem(y + dy, 4)

    def tile(t):
        return pltpu.make_async_remote_copy(
            gains.at[p, q], gains.at[p, q], tile_send.at[t], tile_recv.at[t],
            device_id=(p, at_offset(t // 4, lax.rem(t, 4))), device_id_type=MESH)

    def row(t):
        k = at_offset(t // 4, lax.rem(t, 4))
        return pltpu.make_async_remote_copy(
            spec.at[k], whole.at[:, pl.ds(pl.multiple_of(q * 32, 32), 32), :], row_send.at[t], row_recv.at[t],
            device_id=(p, k), device_id_type=MESH)

    def slab(k, target, t):
        return pltpu.make_async_remote_copy(
            gains.at[k], gains.at[k], slab_send.at[t], slab_recv.at[k],
            device_id=(target, q), device_id_type=MESH)

    each(1, NQ, lambda t: tile(t).start())

    def start_rows():
        for dx, dy in far_first((4, 4), 0):
            row(4 * dx + dy).start()

    @pl.when(core == 0)
    def _():
        start_rows()

    each(1, NQ, lambda t: tile(t).wait())

    each(1, 4, lambda t: slab(p, lax.rem(z + t, 4) * 2, t).start())

    @pl.when(core == 1)
    def _():
        slab(p, p - 1, 0).start()

    @pl.when(core == 0)
    def _():
        each(1, NP, lambda t: slab(lax.rem(p + t, NP), 0, 0).wait_recv())
        each(1, NP, lambda t: slab(lax.rem(p + 1 + t, NP), p + 1, t + 3).start())
        each(1, NQ, lambda t: row(t).wait_send())
        pl.semaphore_signal(turn_sem, inc=1, device_id=(p + 1, q), device_id_type=MESH)

    @pl.when(core == 1)
    def _():
        pl.semaphore_wait(turn_sem, 1)
        start_rows()
        each(1, NP, lambda t: slab(lax.rem(p + t, NP), 0, 0).wait_recv())

    group = lane_group()

    def place(k):
        for h in range(4):
            outs = swap_groups([gains[k, 4 * h + u] for u in range(4)], group)
            for g in range(4):
                index[h, pl.ds(k * 64 + g, 16, stride=4), :] = outs[g]

    each(0, NP, place)
    for a in range(2):
        for b in range(2):
            block = jnp.concatenate([index[2 * a + h, 256 * b : 256 * b + 256, :] for h in range(2)], axis=1).astype(F32).astype(BF16)
            moved = nt(ct[a], block).astype(BF16)
            mirror[256 * a : 256 * a + 256, 256 * b : 256 * b + 256] = nn(moved, ct[b]).astype(jnp.int32)

    def gains_of(i):
        rows = pl.ds(pl.multiple_of(i * 16, 16), 16)
        for o in range(2):
            entries = [0.5 * tab[o, k] for k in range(16)]
            for h in range(4):
                gain[o, rows, 128 * h : 128 * h + 128] = look_up(index[h, rows, :], entries)
            mgain[o, rows, :] = look_up(mirror[rows, :], entries)

    own_rows.wait()
    each(1, NQ, lambda t: row(t).wait_recv())

    @pl.when(core == 1)
    def _():
        each(1, NQ, lambda t: row(t).wait_send())

    def turn(i):
        rows = pl.ds(pl.multiple_of(i * 128, 128), 128)
        for h in range(4):
            at = 128 * h
            real, imag = whole[0, rows, at : at + 128].T, whole[1, rows, at : at + 128].T
            for k, part in enumerate((real, imag, real + imag)):
                high, low = halves(part)
                d[k, at : at + 128, rows] = high
                d[k, SIDE + at : SIDE + at + 128, rows] = low
                d[k, 2 * SIDE + at : 2 * SIDE + at + 128, rows] = high

    each(0, 4, turn)

    def multiply(left):
        one, two, three = (
            nn(jnp.concatenate([high, high, low], axis=1), d[k]) for k, (high, low) in enumerate(left))
        return one - two, three - one - two

    def band(i):
        rows = pl.ds(pl.multiple_of(i * BAND, BAND), BAND)
        lows = pl.ds(pl.multiple_of(SIDE + i * BAND, BAND), BAND)
        for u in range(BAND // 16):
            gains_of(i * (BAND // 16) + u)
        first = multiply([(d[k, rows, :], d[k, lows, :]) for k in range(3)])
        second = multiply([halves(v) for v in (first[0], first[1], first[0] + first[1])])
        for c in range(2):
            direct[c, rows, :] = gain[0, rows, :] * first[c] + gain[1, rows, :] * second[c]
            refl[2 * c, rows, :], refl[2 * c + 1, rows, :] = halves(
                mgain[0, rows, :] * first[c] + mgain[1, rows, :] * second[c])

    each(0, SIDE // BAND, band)
    for a in range(2):
        for b in range(2):
            ra, rb = slice(256 * a, 256 * a + 256), slice(256 * b, 256 * b + 256)
            for c in range(2):
                high = nt(ct[a], refl[2 * c, rb, ra]).astype(BF16)
                low = nt(ct[a], refl[2 * c + 1, rb, ra]).astype(BF16)
                total = direct[c, ra, rb] + (nn(high, ct[b]) + nn(low, ct[b]))
                for h in range(2):
                    both[2 * a + b, c, h] = total[:, 128 * h : 128 * h + 128]

            def pack(i):
                for c in range(2):
                    for h in range(2):
                        outs = swap_groups(
                            [both[2 * a + b, c, h, pl.ds(i * 64 + u, 16, stride=4), :] for u in range(4)], group)
                        for u in range(4):
                            send[4 * a + i, 8 * b + 4 * h + u, 16 * c : 16 * c + 16, :] = outs[u]

            for i in range(4):
                pack(i)

    pl.semaphore_wait(ready_sem, NP - 1)
    mine = pltpu.make_async_copy(send.at[p, q], recv.at[me], out_own)
    mine.start()
    for dx, dy, dz, dc in far_first((4, 4, 4, 2), 2):
        pp = lax.rem(z + dz, 4) * 2 + lax.rem(core + dc, 2)
        qq = at_offset(dx, dy)
        pltpu.make_async_remote_copy(
            send.at[pp, qq], recv.at[me], out_send, out_recv, device_id=(pp, qq), device_id_type=MESH).start()
    each(1, 4, lambda t: slab(p, 0, t).wait_send())

    @pl.when(core == 1)
    def _():
        slab(p, 0, 0).wait_send()

    @pl.when(core == 0)
    def _():
        each(1, NP, lambda t: slab(0, 0, t + 3).wait_send())

    mine.wait()
    most = recv.at[pl.ds(0, NP * NQ - 1)]
    pltpu.make_async_copy(most, most, out_send).wait()
    pltpu.make_async_copy(most, most, out_recv).wait()


BAND = 128
K1_VMEM = 63 << 20


def slot_work(spectra, gindex, partner, table):
    dma = pltpu.SemaphoreType.DMA
    regular = pltpu.SemaphoreType.REGULAR
    return pl.pallas_call(
        slot_kernel,
        out_shape=jax.ShapeDtypeStruct((NP * NQ, 32, 128), F32),
        in_specs=[ANY, ANY, ANY, ANY],
        out_specs=ANY,
        scratch_shapes=[
            pltpu.VMEM((32, 64), jnp.int32),
            pltpu.VMEM((1, SIDE), jnp.int32),
            pltpu.SMEM((2, 16), F32),
            pltpu.VMEM((2, SIDE, SIDE), F32),
            pltpu.VMEM((NP, NQ, 16, 128), jnp.int32),
            pltpu.VMEM((2, 256, 256), BF16),
            pltpu.VMEM((4, SIDE, 128), jnp.int32),
            pltpu.VMEM((SIDE, SIDE), jnp.int32),
            pltpu.VMEM((2, SIDE, SIDE), F32),
            pltpu.VMEM((2, SIDE, SIDE), F32),
            pltpu.VMEM((3, 3 * SIDE, SIDE), BF16),
            pltpu.VMEM((2, SIDE, SIDE), F32),
            pltpu.VMEM((4, SIDE, SIDE), BF16),
            pltpu.VMEM((4, 2, 2, 256, 128), F32),
            pltpu.VMEM((NP, NQ, 32, 128), F32),
            dma((4,)), dma((NQ,)), dma((NQ,)), dma((NQ,)), dma((NQ,)), dma((11,)), dma((NP,)), regular, regular,
            dma, dma, dma,
        ],
        compiler_params=pltpu.CompilerParams(
            collective_id=0, has_side_effects=True, vmem_limit_bytes=K1_VMEM),
        name="slot_work",
    )(spectra, gindex, partner, table)


PART = 16


def time_kernel(counts, recv, table, recorded, out, held, wave_table, rec, res, fetch_sem, table_sem, in_sem, out_sem):
    def load(i):
        at = pl.ds(i * PART, PART)
        return pltpu.make_async_copy(recorded.at[at], rec.at[at], in_sem.at[i])

    def store(i):
        at = pl.ds(i * PART, PART)
        return pltpu.make_async_copy(res.at[at], out.at[at], out_sem.at[i])

    parts = 64 // PART
    row = 0
    for p in range(NP):
        live = counts[p]

        def fetch(k):
            pltpu.make_async_copy(
                recv.at[p * NQ + k], held.at[pl.ds(pl.multiple_of((row + k) * 32, 32), 32), :], fetch_sem).start()

        each(0, live, fetch)
        row = row + live
    basis_copy = pltpu.make_async_copy(table, wave_table, table_sem)
    basis_copy.start()
    each(0, parts, lambda i: load(i).start())
    basis_copy.wait()
    pltpu.make_async_copy(held, held, fetch_sem).wait()

    def part(i):
        load(i).wait()
        chunks = []
        for k in range(PART // 4):
            j = i * (PART // 4) + k
            values = [held[pl.ds(c * 16 + j, LIVE, stride=32), :] for c in range(2)]
            chunks.append(jnp.concatenate(values, axis=0).T)
        high, low = halves(jnp.concatenate(chunks, axis=0))
        wave = nn(jnp.concatenate([high, low, high], axis=1), wave_table[...])
        at = pl.ds(pl.multiple_of(i * PART, PART), PART)
        res[at] = rec[at] - wave.reshape(PART, 32, NT)
        store(i).start()

    each(0, parts, part)
    each(0, parts, lambda i: store(i).wait())


def to_time(counts, recv, table, recorded):
    dma = pltpu.SemaphoreType.DMA
    return pl.pallas_call(
        time_kernel,
        out_shape=jax.ShapeDtypeStruct((64, 32, NT), F32),
        in_specs=[SMEM, ANY, ANY, ANY],
        out_specs=ANY,
        scratch_shapes=[
            pltpu.VMEM((LIVE * 32, 128), F32),
            pltpu.VMEM((6 * LIVE, NT), BF16),
            pltpu.VMEM((64, 32, NT), F32),
            pltpu.VMEM((64, 32, NT), F32),
            dma, dma, dma((64 // PART,)), dma((64 // PART,)),
        ],
        name="to_time",
    )(counts, recv, table, recorded)


def on_device(spectra, counts, partner, recorded, gain_index, gain_table):
    recv = slot_work(spectra, gain_index.T, partner.reshape(1, SIDE), gain_table)
    return to_time(counts, recv, jnp.asarray(basis()), recorded)


def solution(mesh):
    placed = (P("freq", None, "rcv", None), P(), P(), P("freq", "rcv", None), P("freq", "rcv"), P())
    return jax.shard_map(
        on_device, mesh=mesh, in_specs=placed, out_specs=P("freq", "rcv", None), check_vma=False
    )
```

```python
import itertools
import random

import jax
import jax.numpy as jnp
import numpy as np
from jax import lax
from jax.experimental import pallas as pl
from jax.experimental.pallas import tpu as pltpu
from jax.sharding import PartitionSpec as P

MESH = pl.DeviceIdType.MESH
ANY = pl.BlockSpec(memory_space=pl.ANY)
VMEM = pl.BlockSpec(memory_space=pltpu.VMEM)
SMEM = pl.BlockSpec(memory_space=pltpu.SMEM)

NT = 512
SIDE = 512
LIVE = 64
NP = 8
NQ = 16
F32 = jnp.float32
BF16 = jnp.bfloat16


def basis():
    bins = np.arange(1, LIVE + 1, dtype=np.int64)[:, None]
    angles = 2.0 * np.pi / NT * ((bins * np.arange(NT, dtype=np.int64)[None, :]) % NT)
    table = np.concatenate([np.cos(angles), -np.sin(angles)], axis=0).astype(np.float32)
    high = table.astype(BF16)
    low = (table - high.astype(np.float32)).astype(BF16)
    return np.concatenate([high, high, low], axis=0)


def halves(x):
    high = x.astype(BF16)
    return high, (x - high.astype(F32)).astype(BF16)


def lane_group():
    return lax.broadcasted_iota(jnp.int32, (16, 128), 1) // 32


def swap_groups(blocks, group):
    for step in (2, 1):
        upper = (group & step) != 0
        swapped = list(blocks)
        for i in range(4):
            if not i & step:
                low, high = blocks[i], blocks[i + step]
                swapped[i] = jnp.where(upper, pltpu.roll(high, 32 * step, 1), low)
                swapped[i + step] = jnp.where(upper, high, pltpu.roll(low, 128 - 32 * step, 1))
        blocks = swapped
    return blocks


def nt(a, b):
    return lax.dot_general(a, b, (((1,), (1,)), ((), ())), preferred_element_type=F32)


def nn(a, b):
    return jnp.dot(a, b, preferred_element_type=F32)


def look_up(index, entries):
    level = entries
    for bit in range(4):
        odd = (index & (1 << bit)) != 0
        level = [jnp.where(odd, level[2 * k + 1], level[2 * k]) for k in range(len(level) // 2)]
    return level[0]


def each(first, last, fn):
    def body(t, _):
        fn(t)
        return 0

    lax.fori_loop(first, last, body, 0)


def near(offset):
    return sum(min(step, 4 - step) for step in offset[:3])


def far_first(shape, seed):
    offsets = [offset for offset in itertools.product(*map(range, shape)) if any(offset)]
    random.Random(seed).shuffle(offsets)
    return sorted(offsets, key=lambda offset: -near(offset))


def slot_kernel(
    spec, gindex, partner, table, recv,
    gtile, prow, tab, whole, gains, ct, index, mirror, gain, mgain, d, direct, refl, both, send,
    own_sem, row_send, row_recv, tile_send, tile_recv, slab_send, slab_recv, turn_sem, ready_sem,
    out_own, out_send, out_recv,
):
    p, q = lax.axis_index("freq"), lax.axis_index("rcv")
    me = p * NQ + q
    z, core = p // 2, lax.rem(p, 2)
    x, y = q // 4, lax.rem(q, 4)
    mate = p + 1 - 2 * core

    barrier = pltpu.get_barrier_semaphore()

    def greet_q(t):
        pl.semaphore_signal(barrier, inc=1, device_id=(p, lax.rem(q + t, NQ)), device_id_type=MESH)

    def greet_p(t):
        pl.semaphore_signal(barrier, inc=1, device_id=(lax.rem(p + t, NP), q), device_id_type=MESH)

    each(1, NQ, greet_q)
    each(1, NP, greet_p)
    small = [pltpu.make_async_copy(src, dst, own_sem.at[i + 1]) for i, (src, dst) in enumerate(
        ((gindex, gtile), (partner, prow), (table, tab)))]
    for copy in small:
        copy.start()
    own_rows = pltpu.make_async_copy(spec.at[q], whole.at[:, pl.ds(pl.multiple_of(q * 32, 32), 32), :], own_sem.at[0])
    own_rows.start()
    small[0].wait()
    lanes = lax.broadcasted_iota(jnp.int32, (128, 32), 0)
    repeat = (lax.rem(lanes, 32) == lax.broadcasted_iota(jnp.int32, (128, 32), 1)).astype(BF16)
    levels = nn(repeat, gtile[...].astype(F32).astype(BF16))
    sources = lax.broadcasted_iota(jnp.int32, (128, 64), 1)
    groups = lax.broadcasted_iota(jnp.int32, (128, 64), 0) // 32
    levels = jnp.where(lax.rem(sources, 4) == groups, levels, 0.0).astype(BF16)
    fours = lax.broadcasted_iota(jnp.int32, (16, 64), 1) // 4
    fours = (fours == lax.broadcasted_iota(jnp.int32, (16, 64), 0)).astype(BF16)
    gains[p, q] = nt(fours, levels).astype(jnp.int32)
    small[1].wait()
    small[2].wait()
    for b in range(2):
        rows = lax.broadcasted_iota(jnp.int32, (256, 256), 0) + 256 * b
        ct[b] = (rows == prow[:, 256 * b : 256 * b + 256]).astype(F32).T.astype(BF16)
    pl.semaphore_wait(barrier, NQ + NP - 2)
    each(1, NP, lambda t: pl.semaphore_signal(
        ready_sem, inc=1, device_id=(lax.rem(p + t, NP), q), device_id_type=MESH))

    def at_offset(dx, dy):
        return lax.rem(x + dx, 4) * 4 + lax.rem(y + dy, 4)

    def tile(t):
        return pltpu.make_async_remote_copy(
            gains.at[p, q], gains.at[p, q], tile_send.at[t], tile_recv.at[t],
            device_id=(p, at_offset(t // 4, lax.rem(t, 4))), device_id_type=MESH)

    def row(t):
        k = at_offset(t // 4, lax.rem(t, 4))
        return pltpu.make_async_remote_copy(
            spec.at[k], whole.at[:, pl.ds(pl.multiple_of(q * 32, 32), 32), :], row_send.at[t], row_recv.at[t],
            device_id=(p, k), device_id_type=MESH)

    def slab(k, target, t):
        return pltpu.make_async_remote_copy(
            gains.at[k], gains.at[k], slab_send.at[t], slab_recv.at[k],
            device_id=(target, q), device_id_type=MESH)

    each(1, NQ, lambda t: tile(t).start())

    def start_rows():
        for dx, dy in far_first((4, 4), 0):
            row(4 * dx + dy).start()

    @pl.when(core == 0)
    def _():
        start_rows()

    each(1, NQ, lambda t: tile(t).wait())

    each(1, 4, lambda t: slab(p, lax.rem(z + t, 4) * 2, t).start())

    @pl.when(core == 1)
    def _():
        slab(p, p - 1, 0).start()

    @pl.when(core == 0)
    def _():
        each(1, NP, lambda t: slab(lax.rem(p + t, NP), 0, 0).wait_recv())
        each(1, NP, lambda t: slab(lax.rem(p + 1 + t, NP), p + 1, t + 3).start())
        for dx, dy in far_first((4, 4), 0)[:12]:
            row(4 * dx + dy).wait_send()
        pl.semaphore_signal(turn_sem, inc=1, device_id=(p + 1, q), device_id_type=MESH)
        for dx, dy in far_first((4, 4), 0)[12:]:
            row(4 * dx + dy).wait_send()

    @pl.when(core == 1)
    def _():
        pl.semaphore_wait(turn_sem, 1)
        start_rows()
        each(1, NP, lambda t: slab(lax.rem(p + t, NP), 0, 0).wait_recv())

    group = lane_group()

    def place(k):
        for h in range(4):
            outs = swap_groups([gains[k, 4 * h + u] for u in range(4)], group)
            for g in range(4):
                index[h, pl.ds(k * 64 + g, 16, stride=4), :] = outs[g]

    each(0, NP, place)
    for a in range(2):
        for b in range(2):
            block = jnp.concatenate([index[2 * a + h, 256 * b : 256 * b + 256, :] for h in range(2)], axis=1).astype(F32).astype(BF16)
            moved = nt(ct[a], block).astype(BF16)
            mirror[256 * a : 256 * a + 256, 256 * b : 256 * b + 256] = nn(moved, ct[b]).astype(jnp.int32)

    def gains_of(i):
        rows = pl.ds(pl.multiple_of(i * 16, 16), 16)
        for o in range(2):
            entries = [0.5 * tab[o, k] for k in range(16)]
            for h in range(4):
                gain[o, rows, 128 * h : 128 * h + 128] = look_up(index[h, rows, :], entries)
            mgain[o, rows, :] = look_up(mirror[rows, :], entries)

    own_rows.wait()
    each(1, NQ, lambda t: row(t).wait_recv())

    @pl.when(core == 1)
    def _():
        each(1, NQ, lambda t: row(t).wait_send())

    def turn(i):
        rows = pl.ds(128 * i, 128)
        for h in range(4):
            at = 128 * h
            real, imag = whole[0, rows, at : at + 128].T, whole[1, rows, at : at + 128].T
            for k, part in enumerate((real, imag, real + imag)):
                high, low = halves(part)
                d[k, at : at + 128, rows] = high
                d[k, SIDE + at : SIDE + at + 128, rows] = low
                d[k, 2 * SIDE + at : 2 * SIDE + at + 128, rows] = high

    for i in range(4):
        turn(i)

    def multiply(left):
        one, two, three = (
            nn(jnp.concatenate([high, high, low], axis=1), d[k]) for k, (high, low) in enumerate(left))
        return one - two, three - one - two

    def band(i):
        rows = pl.ds(pl.multiple_of(i * BAND, BAND), BAND)
        lows = pl.ds(pl.multiple_of(SIDE + i * BAND, BAND), BAND)
        for u in range(BAND // 16):
            gains_of(i * (BAND // 16) + u)
        first = multiply([(d[k, rows, :], d[k, lows, :]) for k in range(3)])
        second = multiply([halves(v) for v in (first[0], first[1], first[0] + first[1])])
        for c in range(2):
            direct[c, rows, :] = gain[0, rows, :] * first[c] + gain[1, rows, :] * second[c]
            refl[2 * c, rows, :], refl[2 * c + 1, rows, :] = halves(
                mgain[0, rows, :] * first[c] + mgain[1, rows, :] * second[c])

    each(0, SIDE // BAND, band)
    for a in range(2):
        for b in range(2):
            ra, rb = slice(256 * a, 256 * a + 256), slice(256 * b, 256 * b + 256)
            for c in range(2):
                high = nt(ct[a], refl[2 * c, rb, ra]).astype(BF16)
                low = nt(ct[a], refl[2 * c + 1, rb, ra]).astype(BF16)
                total = direct[c, ra, rb] + (nn(high, ct[b]) + nn(low, ct[b]))
                for h in range(2):
                    both[2 * a + b, c, h] = total[:, 128 * h : 128 * h + 128]

            def pack(i):
                for c in range(2):
                    for h in range(2):
                        outs = swap_groups(
                            [both[2 * a + b, c, h, pl.ds(i * 64 + u, 16, stride=4), :] for u in range(4)], group)
                        for u in range(4):
                            send[4 * a + i, 8 * b + 4 * h + u, 16 * c : 16 * c + 16, :] = outs[u]

            for i in range(4):
                pack(i)

    pl.semaphore_wait(ready_sem, NP - 1)
    mine = pltpu.make_async_copy(send.at[p, q], recv.at[me], out_own)
    mine.start()
    for dx, dy, dz, dc in far_first((4, 4, 4, 2), 2):
        pp = lax.rem(z + dz, 4) * 2 + lax.rem(core + dc, 2)
        qq = at_offset(dx, dy)
        pltpu.make_async_remote_copy(
            send.at[pp, qq], recv.at[me], out_send, out_recv, device_id=(pp, qq), device_id_type=MESH).start()
    each(1, 4, lambda t: slab(p, 0, t).wait_send())

    @pl.when(core == 1)
    def _():
        slab(p, 0, 0).wait_send()

    @pl.when(core == 0)
    def _():
        each(1, NP, lambda t: slab(0, 0, t + 3).wait_send())

    mine.wait()
    most = recv.at[pl.ds(0, NP * NQ - 1)]
    pltpu.make_async_copy(most, most, out_send).wait()
    pltpu.make_async_copy(most, most, out_recv).wait()


BAND = 128
K1_VMEM = 63 << 20


def slot_work(spectra, gindex, partner, table):
    dma = pltpu.SemaphoreType.DMA
    regular = pltpu.SemaphoreType.REGULAR
    return pl.pallas_call(
        slot_kernel,
        out_shape=jax.ShapeDtypeStruct((NP * NQ, 32, 128), F32),
        in_specs=[ANY, ANY, ANY, ANY],
        out_specs=ANY,
        scratch_shapes=[
            pltpu.VMEM((32, 64), jnp.int32),
            pltpu.VMEM((1, SIDE), jnp.int32),
            pltpu.SMEM((2, 16), F32),
            pltpu.VMEM((2, SIDE, SIDE), F32),
            pltpu.VMEM((NP, NQ, 16, 128), jnp.int32),
            pltpu.VMEM((2, 256, 256), BF16),
            pltpu.VMEM((4, SIDE, 128), jnp.int32),
            pltpu.VMEM((SIDE, SIDE), jnp.int32),
            pltpu.VMEM((2, SIDE, SIDE), F32),
            pltpu.VMEM((2, SIDE, SIDE), F32),
            pltpu.VMEM((3, 3 * SIDE, SIDE), BF16),
            pltpu.VMEM((2, SIDE, SIDE), F32),
            pltpu.VMEM((4, SIDE, SIDE), BF16),
            pltpu.VMEM((4, 2, 2, 256, 128), F32),
            pltpu.VMEM((NP, NQ, 32, 128), F32),
            dma((4,)), dma((NQ,)), dma((NQ,)), dma((NQ,)), dma((NQ,)), dma((11,)), dma((NP,)), regular, regular,
            dma, dma, dma,
        ],
        compiler_params=pltpu.CompilerParams(
            collective_id=0, has_side_effects=True, vmem_limit_bytes=K1_VMEM),
        name="slot_work",
    )(spectra, gindex, partner, table)


PART = 16


def time_kernel(counts, recv, table, recorded, out, held, wave_table, rec, res, fetch_sem, table_sem, in_sem, out_sem):
    def load(i):
        at = pl.ds(i * PART, PART)
        return pltpu.make_async_copy(recorded.at[at], rec.at[at], in_sem.at[i])

    def store(i):
        at = pl.ds(i * PART, PART)
        return pltpu.make_async_copy(res.at[at], out.at[at], out_sem.at[i])

    parts = 64 // PART
    row = 0
    for p in range(NP):
        live = counts[p]

        pltpu.make_async_copy(
            recv.at[pl.ds(p * NQ * 32, live * 32), :],
            held.at[pl.ds(pl.multiple_of(row * 32, 32), live * 32), :], fetch_sem).start()
        row = row + live
    basis_copy = pltpu.make_async_copy(table, wave_table, table_sem)
    basis_copy.start()
    each(0, parts, lambda i: load(i).start())
    basis_copy.wait()
    pltpu.make_async_copy(held, held, fetch_sem).wait()

    def part(i):
        load(i).wait()
        chunks = []
        for k in range(PART // 4):
            j = i * (PART // 4) + k
            values = [held[pl.ds(c * 16 + j, LIVE, stride=32), :] for c in range(2)]
            chunks.append(jnp.concatenate(values, axis=0).T)
        high, low = halves(jnp.concatenate(chunks, axis=0))
        wave = nn(jnp.concatenate([high, low, high], axis=1), wave_table[...])
        at = pl.ds(pl.multiple_of(i * PART, PART), PART)
        res[at] = rec[at] - wave.reshape(PART, 32, NT)
        store(i).start()

    each(0, parts, part)
    each(0, parts, lambda i: store(i).wait())


def to_time(counts, recv, table, recorded):
    dma = pltpu.SemaphoreType.DMA
    return pl.pallas_call(
        time_kernel,
        out_shape=jax.ShapeDtypeStruct((64, 32, NT), F32),
        in_specs=[SMEM, ANY, ANY, ANY],
        out_specs=ANY,
        scratch_shapes=[
            pltpu.VMEM((LIVE * 32, 128), F32),
            pltpu.VMEM((6 * LIVE, NT), BF16),
            pltpu.VMEM((64, 32, NT), F32),
            pltpu.VMEM((64, 32, NT), F32),
            dma, dma, dma((64 // PART,)), dma((64 // PART,)),
        ],
        name="to_time",
    )(counts, recv.reshape(NP * NQ * 32, 128), table, recorded)


def on_device(spectra, counts, partner, recorded, gain_index, gain_table):
    recv = slot_work(spectra, gain_index.T, partner.reshape(1, SIDE), gain_table)
    return to_time(counts, recv, jnp.asarray(basis()), recorded)


def solution(mesh):
    placed = (P("freq", None, "rcv", None), P(), P(), P("freq", "rcv", None), P("freq", "rcv"), P())
    return jax.shard_map(
        on_device, mesh=mesh, in_specs=placed, out_specs=P("freq", "rcv", None), check_vma=False
    )
```

```python
import itertools
import random

import jax
import jax.numpy as jnp
import numpy as np
from jax import lax
from jax.experimental import pallas as pl
from jax.experimental.pallas import tpu as pltpu
from jax.sharding import PartitionSpec as P

MESH = pl.DeviceIdType.MESH
ANY = pl.BlockSpec(memory_space=pl.ANY)
VMEM = pl.BlockSpec(memory_space=pltpu.VMEM)
SMEM = pl.BlockSpec(memory_space=pltpu.SMEM)

NT = 512
SIDE = 512
LIVE = 64
NP = 8
NQ = 16
F32 = jnp.float32
BF16 = jnp.bfloat16


def basis():
    bins = np.arange(1, LIVE + 1, dtype=np.int64)[:, None]
    angles = 2.0 * np.pi / NT * ((bins * np.arange(NT, dtype=np.int64)[None, :]) % NT)
    table = np.concatenate([np.cos(angles), -np.sin(angles)], axis=0).astype(np.float32)
    high = table.astype(BF16)
    low = (table - high.astype(np.float32)).astype(BF16)
    return np.concatenate([high, high, low], axis=0)


def halves(x):
    high = x.astype(BF16)
    return high, (x - high.astype(F32)).astype(BF16)


def lane_group():
    return lax.broadcasted_iota(jnp.int32, (16, 128), 1) // 32


def swap_groups(blocks, group):
    for step in (2, 1):
        upper = (group & step) != 0
        swapped = list(blocks)
        for i in range(4):
            if not i & step:
                low, high = blocks[i], blocks[i + step]
                swapped[i] = jnp.where(upper, pltpu.roll(high, 32 * step, 1), low)
                swapped[i + step] = jnp.where(upper, high, pltpu.roll(low, 128 - 32 * step, 1))
        blocks = swapped
    return blocks


def nt(a, b):
    return lax.dot_general(a, b, (((1,), (1,)), ((), ())), preferred_element_type=F32)


def nn(a, b):
    return jnp.dot(a, b, preferred_element_type=F32)


def look_up(index, entries):
    level = entries
    for bit in range(4):
        odd = (index & (1 << bit)) != 0
        level = [jnp.where(odd, level[2 * k + 1], level[2 * k]) for k in range(len(level) // 2)]
    return level[0]


def each(first, last, fn):
    def body(t, _):
        fn(t)
        return 0

    lax.fori_loop(first, last, body, 0)


def near(offset):
    return sum(min(step, 4 - step) for step in offset[:3])


def far_first(shape, seed):
    offsets = [offset for offset in itertools.product(*map(range, shape)) if any(offset)]
    random.Random(seed).shuffle(offsets)
    return sorted(offsets, key=lambda offset: -near(offset))


def slot_kernel(
    spec, gindex, partner, table, recv,
    gtile, prow, tab, whole, gains, ct, index, mirror, gain, mgain, d, direct, refl, both, send,
    own_sem, row_send, row_recv, tile_send, tile_recv, slab_send, slab_recv, turn_sem, ready_sem,
    out_own, out_send, out_recv,
):
    p, q = lax.axis_index("freq"), lax.axis_index("rcv")
    me = p * NQ + q
    z, core = p // 2, lax.rem(p, 2)
    x, y = q // 4, lax.rem(q, 4)
    mate = p + 1 - 2 * core

    barrier = pltpu.get_barrier_semaphore()

    def greet_q(t):
        pl.semaphore_signal(barrier, inc=1, device_id=(p, lax.rem(q + t, NQ)), device_id_type=MESH)

    def greet_p(t):
        pl.semaphore_signal(barrier, inc=1, device_id=(lax.rem(p + t, NP), q), device_id_type=MESH)

    each(1, NQ, greet_q)
    each(1, NP, greet_p)
    small = [pltpu.make_async_copy(src, dst, own_sem.at[i + 1]) for i, (src, dst) in enumerate(
        ((gindex, gtile), (partner, prow), (table, tab)))]
    for copy in small:
        copy.start()
    own_rows = pltpu.make_async_copy(spec.at[q], whole.at[:, pl.ds(pl.multiple_of(q * 32, 32), 32), :], own_sem.at[0])
    own_rows.start()
    small[0].wait()
    lanes = lax.broadcasted_iota(jnp.int32, (128, 32), 0)
    repeat = (lax.rem(lanes, 32) == lax.broadcasted_iota(jnp.int32, (128, 32), 1)).astype(BF16)
    levels = nn(repeat, gtile[...].astype(F32).astype(BF16))
    sources = lax.broadcasted_iota(jnp.int32, (128, 64), 1)
    groups = lax.broadcasted_iota(jnp.int32, (128, 64), 0) // 32
    levels = jnp.where(lax.rem(sources, 4) == groups, levels, 0.0).astype(BF16)
    fours = lax.broadcasted_iota(jnp.int32, (16, 64), 1) // 4
    fours = (fours == lax.broadcasted_iota(jnp.int32, (16, 64), 0)).astype(BF16)
    gains[p, q] = nt(fours, levels).astype(jnp.int32)
    small[1].wait()
    small[2].wait()
    for b in range(2):
        rows = lax.broadcasted_iota(jnp.int32, (256, 256), 0) + 256 * b
        ct[b] = (rows == prow[:, 256 * b : 256 * b + 256]).astype(F32).T.astype(BF16)
    pl.semaphore_wait(barrier, NQ + NP - 2)
    each(1, NP, lambda t: pl.semaphore_signal(
        ready_sem, inc=1, device_id=(lax.rem(p + t, NP), q), device_id_type=MESH))

    def at_offset(dx, dy):
        return lax.rem(x + dx, 4) * 4 + lax.rem(y + dy, 4)

    def tile(t):
        return pltpu.make_async_remote_copy(
            gains.at[p, q], gains.at[p, q], tile_send.at[t], tile_recv.at[t],
            device_id=(p, at_offset(t // 4, lax.rem(t, 4))), device_id_type=MESH)

    def row(t):
        k = at_offset(t // 4, lax.rem(t, 4))
        return pltpu.make_async_remote_copy(
            spec.at[k], whole.at[:, pl.ds(pl.multiple_of(q * 32, 32), 32), :], row_send.at[t], row_recv.at[t],
            device_id=(p, k), device_id_type=MESH)

    def slab(k, target, t):
        return pltpu.make_async_remote_copy(
            gains.at[k], gains.at[k], slab_send.at[t], slab_recv.at[k],
            device_id=(target, q), device_id_type=MESH)

    each(1, NQ, lambda t: tile(t).start())

    def start_rows():
        for dx, dy in far_first((4, 4), 0):
            row(4 * dx + dy).start()

    @pl.when(core == 0)
    def _():
        start_rows()

    each(1, NQ, lambda t: tile(t).wait())

    each(1, 4, lambda t: slab(p, lax.rem(z + t, 4) * 2, t).start())

    @pl.when(core == 1)
    def _():
        slab(p, p - 1, 0).start()

    @pl.when(core == 0)
    def _():
        each(1, NP, lambda t: slab(lax.rem(p + t, NP), 0, 0).wait_recv())
        each(1, NP, lambda t: slab(lax.rem(p + 1 + t, NP), p + 1, t + 3).start())
        for dx, dy in far_first((4, 4), 0)[:12]:
            row(4 * dx + dy).wait_send()
        pl.semaphore_signal(turn_sem, inc=1, device_id=(p + 1, q), device_id_type=MESH)
        for dx, dy in far_first((4, 4), 0)[12:]:
            row(4 * dx + dy).wait_send()

    @pl.when(core == 1)
    def _():
        pl.semaphore_wait(turn_sem, 1)
        start_rows()
        each(1, NP, lambda t: slab(lax.rem(p + t, NP), 0, 0).wait_recv())

    group = lane_group()

    def place(k):
        for h in range(4):
            outs = swap_groups([gains[k, 4 * h + u] for u in range(4)], group)
            for g in range(4):
                index[h, pl.ds(k * 64 + g, 16, stride=4), :] = outs[g]

    each(0, NP, place)
    for a in range(2):
        for b in range(2):
            block = jnp.concatenate([index[2 * a + h, 256 * b : 256 * b + 256, :] for h in range(2)], axis=1).astype(F32).astype(BF16)
            moved = nt(ct[a], block).astype(BF16)
            mirror[256 * a : 256 * a + 256, 256 * b : 256 * b + 256] = nn(moved, ct[b]).astype(jnp.int32)

    def gains_of(i):
        rows = pl.ds(pl.multiple_of(i * 16, 16), 16)
        for o in range(2):
            entries = [0.5 * tab[o, k] for k in range(16)]
            for h in range(4):
                gain[o, rows, 128 * h : 128 * h + 128] = look_up(index[h, rows, :], entries)
            mgain[o, rows, :] = look_up(mirror[rows, :], entries)

    own_rows.wait()
    each(1, NQ, lambda t: row(t).wait_recv())

    @pl.when(core == 1)
    def _():
        each(1, NQ, lambda t: row(t).wait_send())

    def turn(i):
        rows = pl.ds(128 * i, 128)
        for h in range(4):
            at = 128 * h
            real, imag = whole[0, rows, at : at + 128].T, whole[1, rows, at : at + 128].T
            for k, part in enumerate((real, imag, real + imag)):
                high, low = halves(part)
                d[k, at : at + 128, rows] = high
                d[k, SIDE + at : SIDE + at + 128, rows] = low
                d[k, 2 * SIDE + at : 2 * SIDE + at + 128, rows] = high

    for i in range(4):
        turn(i)

    def multiply(left):
        one, two, three = (
            nn(jnp.concatenate([high, high, low], axis=1), d[k]) for k, (high, low) in enumerate(left))
        return one - two, three - one - two

    def band(i):
        rows = pl.ds(pl.multiple_of(i * BAND, BAND), BAND)
        lows = pl.ds(pl.multiple_of(SIDE + i * BAND, BAND), BAND)
        for u in range(BAND // 16):
            gains_of(i * (BAND // 16) + u)
        first = multiply([(d[k, rows, :], d[k, lows, :]) for k in range(3)])
        second = multiply([halves(v) for v in (first[0], first[1], first[0] + first[1])])
        for c in range(2):
            direct[c, rows, :] = gain[0, rows, :] * first[c] + gain[1, rows, :] * second[c]
            refl[2 * c, rows, :], refl[2 * c + 1, rows, :] = halves(
                mgain[0, rows, :] * first[c] + mgain[1, rows, :] * second[c])

    each(0, SIDE // BAND, band)
    for a in range(2):
        for b in range(2):
            ra, rb = slice(256 * a, 256 * a + 256), slice(256 * b, 256 * b + 256)
            for c in range(2):
                high = nt(ct[a], refl[2 * c, rb, ra]).astype(BF16)
                low = nt(ct[a], refl[2 * c + 1, rb, ra]).astype(BF16)
                total = direct[c, ra, rb] + (nn(high, ct[b]) + nn(low, ct[b]))
                for h in range(2):
                    both[2 * a + b, c, h] = total[:, 128 * h : 128 * h + 128]

            def pack(i):
                for c in range(2):
                    for h in range(2):
                        outs = swap_groups(
                            [both[2 * a + b, c, h, pl.ds(i * 64 + u, 16, stride=4), :] for u in range(4)], group)
                        for u in range(4):
                            send[4 * a + i, 8 * b + 4 * h + u, 16 * c : 16 * c + 16, :] = outs[u]

            for i in range(4):
                pack(i)

    pl.semaphore_wait(ready_sem, NP - 1)
    mine = pltpu.make_async_copy(send.at[p, q], recv.at[me], out_own)
    mine.start()
    for dx, dy, dz, dc in far_first((4, 4, 4, 2), 9):
        pp = lax.rem(z + dz, 4) * 2 + lax.rem(core + dc, 2)
        qq = at_offset(dx, dy)
        pltpu.make_async_remote_copy(
            send.at[pp, qq], recv.at[me], out_send, out_recv, device_id=(pp, qq), device_id_type=MESH).start()
    each(1, 4, lambda t: slab(p, 0, t).wait_send())

    @pl.when(core == 1)
    def _():
        slab(p, 0, 0).wait_send()

    @pl.when(core == 0)
    def _():
        each(1, NP, lambda t: slab(0, 0, t + 3).wait_send())

    mine.wait()
    most = recv.at[pl.ds(0, NP * NQ - 1)]
    pltpu.make_async_copy(most, most, out_send).wait()
    pltpu.make_async_copy(most, most, out_recv).wait()


BAND = 128
K1_VMEM = 63 << 20


def slot_work(spectra, gindex, partner, table):
    dma = pltpu.SemaphoreType.DMA
    regular = pltpu.SemaphoreType.REGULAR
    return pl.pallas_call(
        slot_kernel,
        out_shape=jax.ShapeDtypeStruct((NP * NQ, 32, 128), F32),
        in_specs=[ANY, ANY, ANY, ANY],
        out_specs=ANY,
        scratch_shapes=[
            pltpu.VMEM((32, 64), jnp.int32),
            pltpu.VMEM((1, SIDE), jnp.int32),
            pltpu.SMEM((2, 16), F32),
            pltpu.VMEM((2, SIDE, SIDE), F32),
            pltpu.VMEM((NP, NQ, 16, 128), jnp.int32),
            pltpu.VMEM((2, 256, 256), BF16),
            pltpu.VMEM((4, SIDE, 128), jnp.int32),
            pltpu.VMEM((SIDE, SIDE), jnp.int32),
            pltpu.VMEM((2, SIDE, SIDE), F32),
            pltpu.VMEM((2, SIDE, SIDE), F32),
            pltpu.VMEM((3, 3 * SIDE, SIDE), BF16),
            pltpu.VMEM((2, SIDE, SIDE), F32),
            pltpu.VMEM((4, SIDE, SIDE), BF16),
            pltpu.VMEM((4, 2, 2, 256, 128), F32),
            pltpu.VMEM((NP, NQ, 32, 128), F32),
            dma((4,)), dma((NQ,)), dma((NQ,)), dma((NQ,)), dma((NQ,)), dma((11,)), dma((NP,)), regular, regular,
            dma, dma, dma,
        ],
        compiler_params=pltpu.CompilerParams(
            collective_id=0, has_side_effects=True, vmem_limit_bytes=K1_VMEM),
        name="slot_work",
    )(spectra, gindex, partner, table)


PART = 16


def time_kernel(counts, recv, table, recorded, out, held, wave_table, rec, res, fetch_sem, table_sem, in_sem, out_sem):
    def load(i):
        at = pl.ds(i * PART, PART)
        return pltpu.make_async_copy(recorded.at[at], rec.at[at], in_sem.at[i])

    def store(i):
        at = pl.ds(i * PART, PART)
        return pltpu.make_async_copy(res.at[at], out.at[at], out_sem.at[i])

    parts = 64 // PART
    row = 0
    for p in range(NP):
        live = counts[p]

        pltpu.make_async_copy(
            recv.at[pl.ds(p * NQ * 32, live * 32), :],
            held.at[pl.ds(pl.multiple_of(row * 32, 32), live * 32), :], fetch_sem).start()
        row = row + live
    basis_copy = pltpu.make_async_copy(table, wave_table, table_sem)
    basis_copy.start()
    each(0, parts, lambda i: load(i).start())
    basis_copy.wait()
    pltpu.make_async_copy(held, held, fetch_sem).wait()

    def part(i):
        load(i).wait()
        chunks = []
        for k in range(PART // 4):
            j = i * (PART // 4) + k
            values = [held[pl.ds(c * 16 + j, LIVE, stride=32), :] for c in range(2)]
            chunks.append(jnp.concatenate(values, axis=0).T)
        high, low = halves(jnp.concatenate(chunks, axis=0))
        wave = nn(jnp.concatenate([high, low, high], axis=1), wave_table[...])
        at = pl.ds(i * PART, PART)
        res[at] = rec[at] - wave.reshape(PART, 32, NT)
        store(i).start()

    for i in range(parts):
        part(i)
    each(0, parts, lambda i: store(i).wait())


def to_time(counts, recv, table, recorded):
    dma = pltpu.SemaphoreType.DMA
    return pl.pallas_call(
        time_kernel,
        out_shape=jax.ShapeDtypeStruct((64, 32, NT), F32),
        in_specs=[SMEM, ANY, ANY, ANY],
        out_specs=ANY,
        scratch_shapes=[
            pltpu.VMEM((LIVE * 32, 128), F32),
            pltpu.VMEM((6 * LIVE, NT), BF16),
            pltpu.VMEM((64, 32, NT), F32),
            pltpu.VMEM((64, 32, NT), F32),
            dma, dma, dma((64 // PART,)), dma((64 // PART,)),
        ],
        name="to_time",
    )(counts, recv.reshape(NP * NQ * 32, 128), table, recorded)


def on_device(spectra, counts, partner, recorded, gain_index, gain_table):
    recv = slot_work(spectra, gain_index.T, partner.reshape(1, SIDE), gain_table)
    return to_time(counts, recv, jnp.asarray(basis()), recorded)


def solution(mesh):
    placed = (P("freq", None, "rcv", None), P(), P(), P("freq", "rcv", None), P("freq", "rcv"), P())
    return jax.shard_map(
        on_device, mesh=mesh, in_specs=placed, out_specs=P("freq", "rcv", None), check_vma=False
    )
```
